128 devices in a mesh: group: 8 (over z, core), patch: 16 (over x, y).
Axes of the slice: x: 4, y: 4, z: 4, core: 2. Of those that a mesh axis runs over, the one named last changes fastest.
Arguments:
- node_latent: bfloat16 [40960, 512], P(('group', 'patch')), may hold values from -6 to 6
- fine_latent: bfloat16 [262144, 512], P(('group', 'patch')), may hold values from -6 to 6
- coarse_latent: bfloat16 [65536, 512], P(('group', 'patch')), may hold values from -6 to 6
- fine_sender: int32 [262144], P(('group', 'patch')), may hold values from 0 to 447
- fine_receiver: int32 [262144], P(('group', 'patch')), may hold values from 0 to 319
- coarse_owner: int32 [65536, 1], P(('group', 'patch')), may hold values from 0 to 127; in each aligned block of 512 rows (0 to 511, 512 to 1023, ...) at most 8 rows name the same one
- coarse_row: int32 [65536], P(('group', 'patch')), may hold values from 0 to 15
- coarse_receiver: int32 [65536], P(('group', 'patch')), may hold values from 0 to 15
- edge_first: bfloat16 [2, 1536, 512], replicated, may hold values from -0.15625 to 0.15625
- edge_bias: float32 [2, 512], replicated, may hold values from -3 to 3
- edge_second: bfloat16 [2, 512, 512], replicated, may hold values from -0.25 to 0.25
- edge_gain: float32 [2, 512], replicated, may hold values from 0.25 to 1.75
- node_first: bfloat16 [2, 1024, 512], replicated, may hold values from -0.1875 to 0.1875
- node_bias: float32 [2, 512], replicated, may hold values from -3 to 3
- node_second: bfloat16 [2, 512, 512], replicated, may hold values from -0.25 to 0.25
- node_gain: float32 [2, 512], replicated, may hold values from 0.25 to 1.75
Outputs:
- node_out: bfloat16 [40960, 512], P(('group', 'patch'))
- fine_out: bfloat16 [262144, 512], P(('group', 'patch'))
- coarse_out: bfloat16 [65536, 512], P(('group', 'patch'))
The draws below stay inside these ranges and needn't reach their ends.
Inputs may be any that keep to these rules, and one draw needn't show every extreme that they name: `fine_sender`: A fine edge's sender indexes the receiving device's patch extended by 64 nodes on each side: values below 64 are the last 64 nodes of the previous patch of the same group, values from 384 on the first 64 nodes of the next patch; patches of a group close into a loop. `coarse_owner`: among the 512 coarse edges of one device, at most 8 have their sender on any one device.
All inputs are finite; a program needn't handle non-finite values.
Results may differ from the reference program's by a relative error of at most 0.0095.
Values may be sent and summed in bfloat16 or wider, within the bound.
A program may use at most 128 MiB of HBM per device.

```python
import math
import jax
import jax.numpy as jnp
import numpy as np
from jax import lax

D = 512
NODE_DEV = 320
FINE_DEV = 2048
CE_DEV = 512
HALO = 64
COARSE = 16
LAYERS = 2
CAP = 8
NODES = 40960
FINE_EDGES = 262144
COARSE_EDGES = 65536
N_GROUP = 8
N_PATCH = 16
DEVICES = 128


def touch_ends(entries, stream_key, least, largest):
    place = [jax.random.randint(jax.random.fold_in(stream_key, axis), (), 0, length) for axis, length in enumerate(entries.shape)]
    main_axis = entries.shape.index(max(entries.shape))
    beside = place[:main_axis] + [(place[main_axis] + 1) % entries.shape[main_axis]] + place[main_axis + 1:]
    return entries.at[tuple(place)].set(least).at[tuple(beside)].set(largest)


def block_levels(key, dims, pieces, low, high):
    def one(dim, parts):
        steps = jax.random.uniform(jax.random.fold_in(jax.random.fold_in(key, 6), dim), (parts,), jnp.float32, low / len(pieces), high / len(pieces))
        return jnp.repeat(jnp.exp(steps), dims[dim] // parts).reshape((-1,) + (1,) * (len(dims) - dim - 1))

    gain = one(*pieces[0])
    for cut in pieces[1:]:
        gain = gain * one(*cut)
    return gain


def deal_out(stream_key, own, number, rows, count, top, most, slope):
    sequence = jax.random.permutation(stream_key, count)
    heavy_load, usual = portions_of(count, rows * top, most, slope, True), portions_of(count, rows * top, most, slope, False)
    places = jnp.arange(count)

    def named(tallies, offset_by):
        used = int((tallies > 0).sum())
        fixed = max(1, used // 4)
        passed = fixed + (places - fixed + offset_by * (used - fixed)) % max(1, count - fixed)
        return jnp.zeros((count,), jnp.int32).at[sequence[jnp.where(places < fixed, places, passed)]].set(jnp.asarray(tallies, jnp.int32))

    tallies = jnp.where(number % 4 == 0, named(heavy_load, number // 4), named(usual, number - number // 4 - 1))
    mixed = jax.random.permutation(jax.random.fold_in(own, 3), count)
    giver, taker = mixed[0:count // 2 * 2:2], mixed[1:count // 2 * 2:2]
    margin = jnp.minimum(tallies[giver] - 1, most - tallies[taker]) // 2
    margin = jnp.where((giver == sequence[0]) | (taker == sequence[0]) | (tallies[taker] == 0), 0, jnp.maximum(margin, 0))
    passed = jax.random.randint(jax.random.fold_in(own, 4), (count // 2,), 0, 1 << 20) % (margin + 1)
    tallies = tallies.at[giver].add(-passed).at[taker].add(passed)
    labels = jnp.searchsorted(jnp.cumsum(tallies), jnp.arange(rows * top), side="right").astype(jnp.int32)
    grid = labels.reshape(top, rows).T
    grid = grid[jax.random.permutation(jax.random.fold_in(own, 1), rows)]
    offset_by = jax.random.randint(jax.random.fold_in(own, 2), (rows, 1), 0, top)
    return jnp.take_along_axis(grid, (jnp.arange(top)[None, :] + offset_by) % top, axis=1)


def portions_of(count, total, reach, lean, full):
    weights = [(1 << 20) // math.isqrt(grade ** lean) + 1 for grade in range(1, count + 1)]
    largest = reach if full else min(reach, max(-(-total // count), total * weights[0] // sum(weights)))
    least = 1 if total - largest >= count - 1 else 0
    holding, spare = [largest] + [least] * (count - 1), total - largest - least * (count - 1)
    while spare > 0:
        movable = [i for i in range(1, count) if holding[i] < largest] or [i for i in range(1, count) if holding[i] < reach]
        pool, left = sum([weights[i] for i in movable]), spare
        for i in movable:
            extra = min(reach - holding[i], max(1, left * weights[i] // pool), spare)
            holding[i] = holding[i] + extra
            spare = spare - extra
    return np.array(holding)


def normal_values(stream_key, extent, width, bound, split=(), held_as=jnp.bfloat16):
    array = jax.random.normal(stream_key, extent, jnp.float32) * width
    if len(split) > 0:
        array = block_levels(stream_key, extent, split, -0.22, 0.18) * array
    return jnp.clip(array, min=-bound, max=bound).astype(held_as)


def setup_inputs(seed: int = 0) -> dict:
    seeds = jax.random.split(jax.random.key(seed), 17)
    node_latent = normal_values(seeds[0], (NODES, D), 1.0, 6.0, ((0, 128),))
    fine_latent = normal_values(seeds[1], (FINE_EDGES, D), 1.0, 6.0, ((0, 128),))
    coarse_latent = normal_values(seeds[2], (COARSE_EDGES, D), 1.0, 6.0, ((0, 128),))
    fine_sender = touch_ends(jax.random.randint(seeds[3], (FINE_EDGES,), 0, NODE_DEV + 2 * HALO), jax.random.fold_in(seeds[3], 1), 0, (NODE_DEV + 2 * HALO) - 1).astype(jnp.int32)
    fine_receiver = touch_ends(jax.random.randint(seeds[4], (FINE_EDGES,), 0, NODE_DEV), jax.random.fold_in(seeds[4], 1), 0, NODE_DEV - 1).astype(jnp.int32)
    coarse_owner_keys = jax.random.split(jax.random.fold_in(seeds[5], 1), COARSE_EDGES // CE_DEV)
    coarse_owner_turns = jax.random.permutation(jax.random.fold_in(seeds[5], 3), COARSE_EDGES // CE_DEV)
    coarse_owner = jax.vmap(lambda own, number: deal_out(jax.random.fold_in(seeds[5], 2), own, number, CE_DEV, DEVICES, 1, CAP, 2))(coarse_owner_keys, coarse_owner_turns).reshape((COARSE_EDGES, 1))
    coarse_row = touch_ends(jax.random.randint(seeds[6], (COARSE_EDGES,), 0, COARSE), jax.random.fold_in(seeds[6], 1), 0, COARSE - 1).astype(jnp.int32)
    coarse_receiver = touch_ends(jax.random.randint(seeds[7], (COARSE_EDGES,), 0, COARSE), jax.random.fold_in(seeds[7], 1), 0, COARSE - 1).astype(jnp.int32)
    edge_first = normal_values(seeds[8], (LAYERS, 3 * D, D), (3 * D) ** -0.5, 0.15625)
    edge_bias = normal_values(seeds[9], (LAYERS, D), 0.5, 3.0, (), jnp.float32)
    edge_second = normal_values(seeds[10], (LAYERS, D, D), D ** -0.5, 0.25)
    edge_gain = jnp.clip(1.0 + 0.15 * jax.random.normal(seeds[11], (LAYERS, D), jnp.float32), 0.25, 1.75)
    node_first = normal_values(seeds[12], (LAYERS, 2 * D, D), (2 * D) ** -0.5, 0.1875)
    node_bias = normal_values(seeds[13], (LAYERS, D), 0.5, 3.0, (), jnp.float32)
    node_second = normal_values(seeds[14], (LAYERS, D, D), D ** -0.5, 0.25)
    node_gain = jnp.clip(1.0 + 0.15 * jax.random.normal(seeds[15], (LAYERS, D), jnp.float32), 0.25, 1.75)
    return {"node_latent": node_latent, "fine_latent": fine_latent, "coarse_latent": coarse_latent, "fine_sender": fine_sender, "fine_receiver": fine_receiver, "coarse_owner": coarse_owner, "coarse_row": coarse_row, "coarse_receiver": coarse_receiver, "edge_first": edge_first, "edge_bias": edge_bias, "edge_second": edge_second, "edge_gain": edge_gain, "node_first": node_first, "node_bias": node_bias, "node_second": node_second, "node_gain": node_gain}


EPSILON = 1e-05

def norm_rows(values, gain_row):
    centre = lax.optimization_barrier(jnp.mean(values, axis=-1, keepdims=True))
    centred = values - centre
    variance = lax.optimization_barrier(jnp.mean(centred * centred, axis=-1, keepdims=True))
    return centred * lax.rsqrt(variance + EPSILON) * gain_row

def edge_block(latent, from_sender, from_receiver, weight_edge, bias_row, weight_second, gain_row):
    pre = jnp.dot(latent, weight_edge, preferred_element_type=jnp.float32) + from_sender + from_receiver + bias_row
    hidden = jax.nn.silu(pre).astype(jnp.bfloat16)
    output = jnp.dot(hidden, weight_second, preferred_element_type=jnp.float32)
    message = norm_rows(output, gain_row)
    updated = (latent.astype(jnp.float32) + message).astype(jnp.bfloat16)
    return (updated, message.astype(jnp.bfloat16))

def reference(node_latent, fine_latent, coarse_latent, fine_sender, fine_receiver, coarse_owner, coarse_row, coarse_receiver, edge_first, edge_bias, edge_second, edge_gain, node_first, node_bias, node_second, node_gain):
    devices = N_GROUP * N_PATCH
    fine_device = jnp.arange(FINE_DEV * devices, dtype=jnp.int32) // FINE_DEV
    group_index = fine_device // N_PATCH
    patch_index = fine_device % N_PATCH
    within = (patch_index * NODE_DEV + fine_sender - HALO) % (N_PATCH * NODE_DEV)
    fine_global = (group_index * (N_PATCH * NODE_DEV) + within).astype(jnp.int32)
    fine_target = (fine_device * NODE_DEV + fine_receiver).astype(jnp.int32)
    coarse_device = jnp.arange(CE_DEV * devices, dtype=jnp.int32) // CE_DEV
    coarse_global = (coarse_owner[:, 0] * NODE_DEV + coarse_row).astype(jnp.int32)
    coarse_target = (coarse_device * NODE_DEV + coarse_receiver).astype(jnp.int32)
    targets = jnp.concatenate([fine_target, coarse_target]).astype(jnp.int32)
    latent = node_latent
    fine_state = fine_latent
    coarse_state = coarse_latent
    for layer_index in range(LAYERS):
        first = edge_first[layer_index]
        weight_edge = first[:D]
        sender_proj = jnp.dot(latent, first[D:2 * D], preferred_element_type=jnp.float32)
        receiver_proj = jnp.dot(latent, first[2 * D:], preferred_element_type=jnp.float32)
        bias_row = edge_bias[layer_index]
        weight_second = edge_second[layer_index]
        gain_row = edge_gain[layer_index]

        def run_block(packed):
            block_latent, block_sender, block_receiver = packed
            return edge_block(block_latent, jnp.take(sender_proj, block_sender, axis=0), jnp.take(receiver_proj, block_receiver, axis=0), weight_edge, bias_row, weight_second, gain_row)
        fine_new, fine_message = lax.map(run_block, (fine_state.reshape(devices, FINE_DEV, D), fine_global.reshape(devices, FINE_DEV), fine_target.reshape(devices, FINE_DEV)))
        coarse_new, coarse_message = lax.map(run_block, (coarse_state.reshape(devices, CE_DEV, D), coarse_global.reshape(devices, CE_DEV), coarse_target.reshape(devices, CE_DEV)))
        fine_state = fine_new.reshape(-1, D)
        coarse_state = coarse_new.reshape(-1, D)
        messages = jnp.concatenate([fine_message.reshape(-1, D), coarse_message.reshape(-1, D)]).astype(jnp.float32)
        summed = jax.ops.segment_sum(messages, targets, num_segments=NODE_DEV * devices).astype(jnp.bfloat16)
        node_weights = node_first[layer_index]
        pre = jnp.dot(latent, node_weights[:D], preferred_element_type=jnp.float32) + jnp.dot(summed, node_weights[D:], preferred_element_type=jnp.float32) + node_bias[layer_index]
        hidden = jax.nn.silu(pre).astype(jnp.bfloat16)
        output = jnp.dot(hidden, node_second[layer_index], preferred_element_type=jnp.float32)
        latent = (latent.astype(jnp.float32) + norm_rows(output, node_gain[layer_index])).astype(jnp.bfloat16)
    return (latent, fine_state, coarse_state)
```

```python
import functools

import jax
import jax.numpy as jnp
from jax import lax
from jax.experimental import pallas as pl
from jax.experimental.pallas import tpu as pltpu
from jax.sharding import PartitionSpec as P

D = 512
NODE = 320
FINE = 2048
CE = 512
HALO = 64
COARSE = 16
LAYERS = 2
PAD = NODE + 2 * HALO
TABLE = PAD + NODE
GATHERED = 128 * COARSE
CHUNK = 256
CHUNKS = FINE // CHUNK
EPSILON = 1e-05
F32 = jnp.float32
BF16 = jnp.bfloat16


def mm(a, b):
    return jnp.dot(a, b, preferred_element_type=F32)


def silu_half(pre):
    u = pre * 0.5
    return (u + u * jnp.tanh(u)).astype(BF16)


def norm_rows(values, gain_row):
    centred = values - jnp.mean(values, axis=-1, keepdims=True)
    variance = jnp.mean(centred * centred, axis=-1, keepdims=True)
    return centred * lax.rsqrt(variance + EPSILON) * gain_row


def onehot(cond):
    return jnp.where(cond, 1.0, 0.0).astype(BF16)


def column(row):
    return jnp.transpose(jnp.broadcast_to(row, (128, 128)))


def kernel(
    h_hbm, fine_hbm, coarse_hbm, fs, fr, co, cr, cv, ef_hbm, eb, e2_hbm, eg, nf_hbm, nb, n2_hbm, ng,
    node_out, fine_out, coarse_out,
    L, ohT, CL, coh, crh, cohT, R, Wsr, W2, Nf, N2, H, halo, T, agg, pc, pn,
    lsem, fsem, osem, ssem, rsem,
    *, comm,
):
    loads = {
        "h": pltpu.make_async_copy(h_hbm, H.at[0], lsem.at[0]),
        "wsr0": pltpu.make_async_copy(ef_hbm.at[0, pl.ds(D, 2 * D)], Wsr.at[0], lsem.at[1]),
        "r0": pltpu.make_async_copy(ef_hbm.at[0, pl.ds(0, D)], R.at[0, pl.ds(0, D)], lsem.at[2]),
        "w2": pltpu.make_async_copy(e2_hbm, W2, lsem.at[3]),
        "nf": pltpu.make_async_copy(nf_hbm, Nf, lsem.at[4]),
        "coarse": pltpu.make_async_copy(coarse_hbm, CL, lsem.at[5]),
        "n2": pltpu.make_async_copy(n2_hbm, N2, lsem.at[6]),
        "wsr1": pltpu.make_async_copy(ef_hbm.at[1, pl.ds(D, 2 * D)], Wsr.at[1], lsem.at[7]),
        "r1": pltpu.make_async_copy(ef_hbm.at[1, pl.ds(0, D)], R.at[1, pl.ds(0, D)], lsem.at[8]),
    }

    def fine_load(i):
        rows = pl.ds(pl.multiple_of(i * CHUNK, CHUNK), CHUNK)
        return pltpu.make_async_copy(fine_hbm.at[rows], L.at[rows, pl.ds(0, D)], fsem.at[i])

    def fine_store(i):
        rows = pl.ds(pl.multiple_of(i * CHUNK, CHUNK), CHUNK)
        return pltpu.make_async_copy(L.at[rows, pl.ds(0, D)], fine_out.at[rows], fsem.at[CHUNKS + i])

    loads["h"].start()
    loads["wsr0"].start()
    loads["r0"].start()
    fine_load(0).start()
    fine_load(1).start()
    loads["w2"].start()
    for i in range(2, CHUNKS):
        fine_load(i).start()
    for name in ("coarse", "nf", "n2", "wsr1", "r1"):
        loads[name].start()

    if comm:
        group = lax.axis_index("group")
        patch = lax.axis_index("patch")
        z, c = group // 2, group % 2
        x, y = patch // 4, patch % 4
        i1 = (1 - c) * y + c * z
        i2 = (1 - c) * x + c * y
        i3 = (1 - c) * z + c * x

        def device(j1, j2, j3, core):
            jy = (1 - c) * j1 + c * j2
            jx = (1 - c) * j2 + c * j3
            jz = (1 - c) * j3 + c * j1
            return {"group": jz * 2 + core, "patch": jx * 4 + jy}

        def base(j1, j2, j3):
            return pl.multiple_of((((c * 4 + j3) * 4 + j2) * 4 + j1) * COARSE, COARSE)

        def turn(i, k):
            return (i + k) % 4

        stage1 = [device(turn(i1, k), i2, i3, c) for k in (1, 3, 2)]
        stage2 = [device(i1, turn(i2, k), i3, c) for k in (1, 3, 2)]
        right, left = (device(i1, i2, turn(i3, k), c) for k in (1, 3))
        partner = {"group": z * 2 + (1 - c), "patch": patch}
        following = {"group": group, "patch": (patch + 1) % 16}
        previous = {"group": group, "patch": (patch + 15) % 16}

        def remote(l, k, src, dst, target):
            return pltpu.make_async_remote_copy(
                src_ref=src, dst_ref=dst, send_sem=ssem.at[l, k], recv_sem=rsem.at[l, k],
                device_id=target, device_id_type=pl.DeviceIdType.MESH,
            )

        def same(l, k, start, count, target):
            ref = T.at[l, pl.ds(start, count)]
            return remote(l, k, ref, ref, target)

        def halos(l):
            return [
                remote(l, 0, H.at[l, pl.ds(NODE - HALO, HALO)], halo.at[l, pl.ds(0, HALO)], following),
                remote(l, 1, H.at[l, pl.ds(0, HALO)], halo.at[l, pl.ds(HALO, HALO)], previous),
            ]

        def own(l):
            return pltpu.make_async_copy(
                H.at[l, pl.ds(0, COARSE)], T.at[l, pl.ds(base(i1, i2, i3), COARSE)], osem.at[2 + l]
            )

        def gather1(l):
            return [
                remote(l, 2 + k, H.at[l, pl.ds(0, COARSE)], T.at[l, pl.ds(base(i1, i2, i3), COARSE)], to)
                for k, to in enumerate(stage1)
            ]

        def gather2(l):
            return [same(l, 5 + k, base(0, i2, i3), 4 * COARSE, to) for k, to in enumerate(stage2)]

        def gather3(l):
            half_a, half_b = base(0, 0, i3), base(0, 2, i3)
            return [
                same(l, 8, half_a, 128, right),
                same(l, 9, half_b, 128, left),
                same(l, 10, half_b, 128, right),
                same(l, 11, half_a, 128, left),
            ]

        def relays(l):
            return [
                same(l, 12, base(0, 0, turn(i3, 3)), 128, right),
                same(l, 13, base(0, 2, turn(i3, 1)), 128, left),
            ]

        def across(l):
            return [
                same(l, 14, base(0, 0, i3), 256, partner),
                same(l, 15, base(0, 0, turn(i3, 3)), 256, partner),
                same(l, 16, base(0, 0, turn(i3, 1)), 256, partner),
                same(l, 17, base(0, 0, turn(i3, 2)), 128, partner),
                same(l, 18, base(0, 2, turn(i3, 2)), 128, partner),
            ]

        barrier = pltpu.get_barrier_semaphore()
        peers = [*stage1, *stage2, right, left, partner, following, previous]
        for peer in peers:
            pl.semaphore_signal(barrier, inc=1, device_id=peer, device_id_type=pl.DeviceIdType.MESH)

        def begin(l):
            for copy in [*gather1(l), *halos(l), own(l)]:
                copy.start()

        def step1(l):
            for copy in gather1(l):
                copy.wait_recv()
            own(l).wait()
            for copy in gather2(l):
                copy.start()

        def step2(l):
            for copy in gather2(l):
                copy.wait_recv()
            for copy in [*gather3(l), across(l)[0]]:
                copy.start()

        def step3(l):
            sent = gather3(l)
            sent[0].wait_recv()
            relays(l)[0].start()
            sent[1].wait_recv()
            relays(l)[1].start()

        def step4(l):
            sent = gather3(l)
            sent[2].wait_recv()
            across(l)[1].start()
            sent[3].wait_recv()
            across(l)[2].start()

        def step5(l):
            for k in range(2):
                relays(l)[k].wait_recv()
                across(l)[3 + k].start()

        def finish(l):
            for copy in across(l):
                copy.wait_recv()
            for copy in [*halos(l), *gather1(l), *gather2(l), *gather3(l), *relays(l), *across(l)]:
                copy.wait_send()

        def wait_halos(l):
            for copy in halos(l):
                copy.wait_recv()
    else:
        begin = step1 = step2 = step3 = step4 = step5 = finish = wait_halos = lambda l: None

    lane = lax.broadcasted_iota(jnp.int32, (128, 128), 1)
    row_node = lax.broadcasted_iota(jnp.int32, (NODE, 128), 0)

    def build_fine(k, carry):
        sender = column(fs[pl.ds(k, 1), :])
        receiver_row = fr[pl.ds(k, 1), :]
        receiver = column(receiver_row) + PAD
        rows = pl.ds(pl.multiple_of(k * 128, 128), 128)
        for b in range(TABLE // 128):
            at = lane + b * 128
            if b < 3:
                cond = sender == at
            elif b == 3:
                cond = (sender == at) | (receiver == at)
            else:
                cond = receiver == at
            L[rows, D + b * 128 : D + (b + 1) * 128] = onehot(cond)
        ohT[:, rows] = onehot(row_node == receiver_row)
        return carry

    def build_coarse(k, carry):
        owner = co[pl.ds(k, 1), :]
        oz, oc, ox, oy = owner >> 5, (owner >> 4) & 1, (owner >> 2) & 3, owner & 3
        block0 = oz * 16 + ox * 4 + oy
        block1 = 64 + ox * 16 + oy * 4 + oz
        block = (1 - oc) * block0 + oc * block1
        sender = column(block * COARSE + cr[pl.ds(k, 1), :])
        receiver_row = cv[pl.ds(k, 1), :]
        rows = pl.ds(pl.multiple_of(k * 128, 128), 128)
        for b in range(GATHERED // 128):
            coh[rows, b * 128 : (b + 1) * 128] = onehot(sender == lane + b * 128)
        crh[rows, :] = onehot(column(receiver_row) == lane)
        cohT[:, rows] = onehot(lax.broadcasted_iota(jnp.int32, (COARSE, 128), 0) == receiver_row)
        return carry

    loads["h"].wait()
    if comm:
        pl.semaphore_wait(barrier, len(peers))
    begin(0)
    lax.fori_loop(0, FINE // 128, build_fine, 0)
    loads["wsr0"].wait()

    def fine_chunk(l, i):
        rows = pl.ds(pl.multiple_of(i * CHUNK, CHUNK), CHUNK)
        hidden = silu_half(mm(L[rows, :], R[l]))
        message = norm_rows(mm(hidden, W2[l]), eg[pl.ds(l, 1), :])
        L[rows, 0:D] = (L[rows, 0:D].astype(F32) + message).astype(BF16)
        agg[...] += mm(ohT[:, rows], message.astype(BF16))

    def layer(l, carry):
        latent = H[l]
        R[l, D + HALO : D + HALO + NODE] = mm(latent, Wsr[l, 0:D]).astype(BF16)
        R[l, D + PAD : D + TABLE] = (mm(latent, Wsr[l, D : 2 * D]) + eb[pl.ds(l, 1), :]).astype(BF16)
        agg[...] = jnp.zeros_like(agg)
        step1(l)
        wait_halos(l)
        ends = mm(halo[l], Wsr[l, 0:D]).astype(BF16)
        R[l, D : D + HALO] = ends[0:HALO]
        R[l, D + HALO + NODE : D + PAD] = ends[HALO : 2 * HALO]

        @pl.when(l == 0)
        def _():
            loads["r0"].wait()
            loads["w2"].wait()

        def chunk_step(i, inner):
            @pl.when(i == 2)
            def _():
                step2(l)

            @pl.when(i == 5)
            def _():
                step3(l)

            @pl.when(i == 7)
            def _():
                step4(l)

            @pl.when(l == 0)
            def _():
                fine_load(i).wait()

            fine_chunk(l, i)

            @pl.when(l == LAYERS - 1)
            def _():
                fine_store(i).start()

            return inner

        lax.fori_loop(0, CHUNKS, chunk_step, 0)

        @pl.when(l == 0)
        def _():
            lax.fori_loop(0, CE // 128, build_coarse, 0)
            for name in ("coarse", "nf", "n2", "wsr1", "r1"):
                loads[name].wait()

        pc[...] = mm(CL[...], R[l, 0:D]) + mm(crh[...], R[l, D + PAD : D + PAD + 128])
        step5(l)
        pn[...] = mm(latent, Nf[l, 0:D]) + nb[pl.ds(l, 1), :]
        finish(l)

        sender = mm(coh[...], T[l]).astype(BF16)
        hidden = silu_half(pc[...] + mm(sender, Wsr[l, 0:D]))
        message = norm_rows(mm(hidden, W2[l]), eg[pl.ds(l, 1), :])
        CL[...] = (CL[...].astype(F32) + message).astype(BF16)

        @pl.when(l == LAYERS - 1)
        def _():
            pltpu.make_async_copy(CL, coarse_out, osem.at[0]).start()

        agg[0:COARSE, :] += mm(cohT[...], message.astype(BF16))
        node_hidden = silu_half(pn[...] + mm(agg[...].astype(BF16), Nf[l, D : 2 * D]))
        update = norm_rows(mm(node_hidden, N2[l]), ng[pl.ds(l, 1), :])
        H[l + 1] = (latent.astype(F32) + update).astype(BF16)

        @pl.when(l < LAYERS - 1)
        def _():
            begin(l + 1)

        return carry

    lax.fori_loop(0, LAYERS, layer, 0)
    last = pltpu.make_async_copy(H.at[LAYERS], node_out, osem.at[1])
    last.start()
    for i in range(CHUNKS):
        fine_store(i).wait()
    pltpu.make_async_copy(CL, coarse_out, osem.at[0]).wait()
    last.wait()


def call(comm, *args):
    (node, fine, coarse, fs, fr, co, cr, cv, ef, eb, e2, eg, nf, nb, n2, ng) = args
    anyspec = pl.BlockSpec(memory_space=pl.ANY)
    vmem = pl.BlockSpec(memory_space=pltpu.VMEM)
    copies = 19
    return pl.pallas_call(
        functools.partial(kernel, comm=comm),
        name="processor",
        out_shape=(
            jax.ShapeDtypeStruct((NODE, D), BF16),
            jax.ShapeDtypeStruct((FINE, D), BF16),
            jax.ShapeDtypeStruct((CE, D), BF16),
        ),
        in_specs=[anyspec] * 3 + [vmem] * 5 + [anyspec, vmem, anyspec, vmem] * 2,
        out_specs=(anyspec, anyspec, anyspec),
        scratch_shapes=[
            pltpu.VMEM((FINE, D + TABLE), BF16),
            pltpu.VMEM((NODE, FINE), BF16),
            pltpu.VMEM((CE, D), BF16),
            pltpu.VMEM((CE, GATHERED), BF16),
            pltpu.VMEM((CE, 128), BF16),
            pltpu.VMEM((COARSE, CE), BF16),
            pltpu.VMEM((LAYERS, D + TABLE, D), BF16),
            pltpu.VMEM((LAYERS, 2 * D, D), BF16),
            pltpu.VMEM((LAYERS, D, D), BF16),
            pltpu.VMEM((LAYERS, 2 * D, D), BF16),
            pltpu.VMEM((LAYERS, D, D), BF16),
            pltpu.VMEM((LAYERS + 1, NODE, D), BF16),
            pltpu.VMEM((LAYERS, 2 * HALO, D), BF16),
            pltpu.VMEM((LAYERS, GATHERED, D), BF16),
            pltpu.VMEM((NODE, D), F32),
            pltpu.VMEM((CE, D), F32),
            pltpu.VMEM((NODE, D), F32),
            pltpu.SemaphoreType.DMA((9,)),
            pltpu.SemaphoreType.DMA((2 * CHUNKS,)),
            pltpu.SemaphoreType.DMA((4,)),
            pltpu.SemaphoreType.DMA((LAYERS, copies)),
            pltpu.SemaphoreType.DMA((LAYERS, copies)),
        ],
        compiler_params=pltpu.CompilerParams(
            collective_id=0 if comm else None, has_side_effects=True, vmem_limit_bytes=56 * 1024 * 1024
        ),
    )(
        node, fine, coarse,
        fs.reshape(FINE // 128, 128), fr.reshape(FINE // 128, 128),
        co.reshape(CE // 128, 128), cr.reshape(CE // 128, 128), cv.reshape(CE // 128, 128),
        ef, eb, e2, eg, nf, nb, n2, ng,
    )


def solution(mesh):
    rows = P(("group", "patch"), None)
    flat = P(("group", "patch"))
    in_specs = (rows, rows, rows, flat, flat, rows, flat, flat) + (P(),) * 8
    return jax.shard_map(
        functools.partial(call, True), mesh=mesh, in_specs=in_specs, out_specs=(rows, rows, rows), check_vma=False
    )
```

```python
import functools

import jax
import jax.numpy as jnp
from jax import lax
from jax.experimental import pallas as pl
from jax.experimental.pallas import tpu as pltpu
from jax.sharding import PartitionSpec as P

D = 512
NODE = 320
FINE = 2048
CE = 512
HALO = 64
COARSE = 16
LAYERS = 2
PAD = NODE + 2 * HALO
TABLE = PAD + NODE
GATHERED = 128 * COARSE
CHUNK = 512
CHUNKS = FINE // CHUNK
EPSILON = 1e-05
F32 = jnp.float32
BF16 = jnp.bfloat16


def mm(a, b):
    return jnp.dot(a, b, preferred_element_type=F32)


def silu_half(pre):
    u = pre * 0.5
    return (u + u * jnp.tanh(u)).astype(BF16)


def norm_rows(values, gain_row):
    centred = values - jnp.mean(values, axis=-1, keepdims=True)
    variance = jnp.mean(centred * centred, axis=-1, keepdims=True)
    return centred * lax.rsqrt(variance + EPSILON) * gain_row


def onehot(cond):
    return jnp.where(cond, 1.0, 0.0).astype(BF16)


def column(row):
    return jnp.transpose(jnp.broadcast_to(row, (128, 128)))


def kernel(
    h_hbm, fine_hbm, coarse_hbm, fs, fr, co, cr, cv, ef_hbm, eb, e2_hbm, eg, nf_hbm, nb, n2_hbm, ng,
    node_out, fine_out, coarse_out,
    L, ohT, CL, coh, crh, cohT, R, Wsr, W2, Nf, N2, H, halo, T, agg, pc, pn,
    lsem, fsem, osem, ssem, rsem,
    *, comm,
):
    loads = {
        "h": pltpu.make_async_copy(h_hbm, H.at[0], lsem.at[0]),
        "wsr0": pltpu.make_async_copy(ef_hbm.at[0, pl.ds(D, 2 * D)], Wsr.at[0], lsem.at[1]),
        "r0": pltpu.make_async_copy(ef_hbm.at[0, pl.ds(0, D)], R.at[0, pl.ds(0, D)], lsem.at[2]),
        "w2": pltpu.make_async_copy(e2_hbm, W2, lsem.at[3]),
        "nf": pltpu.make_async_copy(nf_hbm, Nf, lsem.at[4]),
        "coarse": pltpu.make_async_copy(coarse_hbm, CL, lsem.at[5]),
        "n2": pltpu.make_async_copy(n2_hbm, N2, lsem.at[6]),
        "wsr1": pltpu.make_async_copy(ef_hbm.at[1, pl.ds(D, 2 * D)], Wsr.at[1], lsem.at[7]),
        "r1": pltpu.make_async_copy(ef_hbm.at[1, pl.ds(0, D)], R.at[1, pl.ds(0, D)], lsem.at[8]),
    }

    def fine_load(i):
        rows = pl.ds(pl.multiple_of(i * CHUNK, CHUNK), CHUNK)
        return pltpu.make_async_copy(fine_hbm.at[rows], L.at[rows, pl.ds(0, D)], fsem.at[i])

    def fine_store(i):
        rows = pl.ds(pl.multiple_of(i * CHUNK, CHUNK), CHUNK)
        return pltpu.make_async_copy(L.at[rows, pl.ds(0, D)], fine_out.at[rows], fsem.at[CHUNKS + i])

    loads["h"].start()
    loads["wsr0"].start()
    loads["r0"].start()
    fine_load(0).start()
    fine_load(1).start()
    loads["w2"].start()
    for i in range(2, CHUNKS):
        fine_load(i).start()
    for name in ("coarse", "nf", "n2", "wsr1", "r1"):
        loads[name].start()

    if comm:
        group = lax.axis_index("group")
        patch = lax.axis_index("patch")
        z, c = group // 2, group % 2
        x, y = patch // 4, patch % 4
        here = (x, y, z)

        def swap1(i):
            return i + 1 - 2 * (i % 2)

        def swap3(i):
            return 3 - i

        def cube(swap):
            targets = []
            for mask in range(1, 8):
                tx, ty, tz = (swap(i) if mask >> k & 1 else i for k, i in enumerate(here))
                targets.append({"group": tz * 2 + c, "patch": tx * 4 + ty})
            return targets

        near, far = cube(swap1), cube(swap3)
        first, second = (near, far), (far, near)
        partner = {"group": z * 2 + (1 - c), "patch": patch}
        following = {"group": group, "patch": (patch + 1) % 16}
        previous = {"group": group, "patch": (patch + 15) % 16}

        def bundle(side):
            pair = [(i + side) // 2 % 2 for i in here]
            return ((c * 2 + side) * 8 + pair[0] * 4 + pair[1] * 2 + pair[2]) * 64

        within = ((x % 2) * 4 + (y % 2) * 2 + z % 2) * 8

        def remote(l, k, src, dst, target):
            return pltpu.make_async_remote_copy(
                src_ref=src, dst_ref=dst, send_sem=ssem.at[l, k], recv_sem=rsem.at[l, k],
                device_id=target, device_id_type=pl.DeviceIdType.MESH,
            )

        def same(l, k, start, count, target):
            ref = T.at[l, pl.ds(pl.multiple_of(start, 8), count)]
            return remote(l, k, ref, ref, target)

        def halos(l):
            return [
                remote(l, 0, H.at[l, pl.ds(NODE - HALO, HALO)], halo.at[l, pl.ds(0, HALO)], following),
                remote(l, 1, H.at[l, pl.ds(0, HALO)], halo.at[l, pl.ds(HALO, HALO)], previous),
            ]

        def own(l, side):
            dst = T.at[l, pl.ds(pl.multiple_of(bundle(side) + within, 8), 8)]
            return H.at[l, pl.ds(side * 8, 8)], dst

        def exchange(l):
            return same(l, 4, c * 1024, 1024, partner)

        barrier = pltpu.get_barrier_semaphore()
        peers = [*near, *far, partner, following, previous]
        for peer in peers:
            pl.semaphore_signal(barrier, inc=1, device_id=peer, device_id_type=pl.DeviceIdType.MESH)

        def begin(l):
            for side in range(2):
                for target in first[side]:
                    remote(l, 2, *own(l, side), target).start()
            for side in range(2):
                pltpu.make_async_copy(*own(l, side), osem.at[2 + 2 * l + side]).start()
            for copy in halos(l):
                copy.start()

        def step1(l):
            same(l, 2, 0, 14 * 8, partner).wait_recv()
            for side in range(2):
                pltpu.make_async_copy(*own(l, side), osem.at[2 + 2 * l + side]).wait()
            for side in range(2):
                for target in second[side]:
                    same(l, 3, bundle(side), 64, target).start()

        def step2(l):
            same(l, 3, 0, 14 * 64, partner).wait_recv()
            exchange(l).start()

        def finish(l):
            exchange(l).wait_recv()

        def drain(l):
            same(l, 2, 0, 14 * 8, partner).wait_send()
            same(l, 3, 0, 14 * 64, partner).wait_send()
            for copy in [*halos(l), exchange(l)]:
                copy.wait_send()

        def wait_halos(l):
            for copy in halos(l):
                copy.wait_recv()
    else:
        c = 0
        begin = step1 = step2 = finish = drain = wait_halos = lambda l: None

    lane = lax.broadcasted_iota(jnp.int32, (128, 128), 1)
    row_node = lax.broadcasted_iota(jnp.int32, (NODE, 128), 0)

    def build_fine(k, carry):
        sender = column(fs[pl.ds(k, 1), :])
        receiver_row = fr[pl.ds(k, 1), :]
        receiver = column(receiver_row) + PAD
        rows = pl.ds(pl.multiple_of(k * 128, 128), 128)
        for b in range(TABLE // 128):
            at = lane + b * 128
            if b < 3:
                cond = sender == at
            elif b == 3:
                cond = (sender == at) | (receiver == at)
            else:
                cond = receiver == at
            L[rows, D + b * 128 : D + (b + 1) * 128] = onehot(cond)
        ohT[:, rows] = onehot(row_node == receiver_row)
        return carry

    def build_coarse(k, carry):
        owner = co[pl.ds(k, 1), :]
        row = cr[pl.ds(k, 1), :]
        oz, oc, ox, oy = owner >> 5, (owner >> 4) & 1, (owner >> 2) & 3, owner & 3
        side = row >> 3
        px, py, pz = (((i + side) >> 1) & 1 for i in (ox, oy, oz))
        place = ((px * 2 + py) * 2 + pz) * 8 + ((ox & 1) * 2 + (oy & 1)) * 2 + (oz & 1)
        sender = column(((oc * 2 + side) * 64 + place) * 8 + (row & 7))
        receiver_row = cv[pl.ds(k, 1), :]
        rows = pl.ds(pl.multiple_of(k * 128, 128), 128)
        for b in range(GATHERED // 128):
            coh[rows, b * 128 : (b + 1) * 128] = onehot(sender == lane + b * 128)
        crh[rows, :] = onehot(column(receiver_row) == lane)
        cohT[:, rows] = onehot(lax.broadcasted_iota(jnp.int32, (COARSE, 128), 0) == receiver_row)
        return carry

    loads["h"].wait()
    if comm:
        pl.semaphore_wait(barrier, len(peers))
    begin(0)
    lax.fori_loop(0, FINE // 128, build_fine, 0)
    loads["wsr0"].wait()

    def fine_chunk(l, i):
        rows = pl.ds(pl.multiple_of(i * CHUNK, CHUNK), CHUNK)
        hidden = silu_half(mm(L[rows, :], R[l]))
        message = norm_rows(mm(hidden, W2[l]), eg[pl.ds(l, 1), :])
        L[rows, 0:D] = (L[rows, 0:D].astype(F32) + message).astype(BF16)
        agg[...] += mm(ohT[:, rows], message.astype(BF16))

    def node_rows(l, start, count, received):
        rows = slice(start, start + count)
        hidden = silu_half(pn[rows] + mm(received.astype(BF16), Nf[l, D : 2 * D]))
        update = norm_rows(mm(hidden, N2[l]), ng[pl.ds(l, 1), :])
        H[l + 1, rows] = (H[l, rows].astype(F32) + update).astype(BF16)

    def layer(l, carry):
        latent = H[l]
        R[l, D + HALO : D + HALO + NODE] = mm(latent, Wsr[l, 0:D]).astype(BF16)
        R[l, D + PAD : D + TABLE] = (mm(latent, Wsr[l, D : 2 * D]) + eb[pl.ds(l, 1), :]).astype(BF16)
        agg[...] = jnp.zeros_like(agg)
        wait_halos(l)
        ends = mm(halo[l], Wsr[l, 0:D]).astype(BF16)
        R[l, D : D + HALO] = ends[0:HALO]
        R[l, D + HALO + NODE : D + PAD] = ends[HALO : 2 * HALO]
        step1(l)

        @pl.when(l == 0)
        def _():
            loads["r0"].wait()
            loads["w2"].wait()

        def chunk_step(i, inner):
            @pl.when(l == 0)
            def _():
                fine_load(i).wait()

            fine_chunk(l, i)

            @pl.when(l == LAYERS - 1)
            def _():
                fine_store(i).start()

            return inner

        lax.fori_loop(0, CHUNKS, chunk_step, 0)

        @pl.when(l == 0)
        def _():
            lax.fori_loop(0, CE // 128, build_coarse, 0)
            for name in ("coarse", "nf", "n2", "wsr1", "r1"):
                loads[name].wait()

        pc[...] = mm(CL[...], R[l, 0:D]) + mm(crh[...], R[l, D + PAD : D + PAD + 128])
        pn[...] = mm(latent, Nf[l, 0:D]) + nb[pl.ds(l, 1), :]
        node_rows(l, COARSE, NODE - COARSE, agg[COARSE:NODE])
        step2(l)
        mine = pl.ds(pl.multiple_of(c * 1024, 1024), 1024)
        other = pl.ds(pl.multiple_of((1 - c) * 1024, 1024), 1024)
        sender = mm(coh[:, mine], T[l, mine])
        finish(l)
        sender = (sender + mm(coh[:, other], T[l, other])).astype(BF16)
        hidden = silu_half(pc[...] + mm(sender, Wsr[l, 0:D]))
        message = norm_rows(mm(hidden, W2[l]), eg[pl.ds(l, 1), :])
        node_rows(l, 0, COARSE, agg[0:COARSE] + mm(cohT[...], message.astype(BF16)))

        @pl.when(l < LAYERS - 1)
        def _():
            begin(l + 1)

        CL[...] = (CL[...].astype(F32) + message).astype(BF16)
        drain(l)
        return carry

    lax.fori_loop(0, LAYERS, layer, 0)
    finals = [
        pltpu.make_async_copy(CL, coarse_out, osem.at[0]),
        pltpu.make_async_copy(H.at[LAYERS], node_out, osem.at[1]),
    ]
    for copy in finals:
        copy.start()
    for i in range(CHUNKS):
        fine_store(i).wait()
    for copy in finals:
        copy.wait()


def hand_over(node, fine, coarse, node_out, fine_out, coarse_out, N, F, C, sem):
    pieces = [(coarse, C, coarse_out, 0, CE), (node, N, node_out, 0, NODE)]
    pieces += [(fine, F, fine_out, k * 512, 512) for k in range(FINE // 512)]
    arrive, leave = [], []
    for k, (src, buffer, dst, start, count) in enumerate(pieces):
        rows = pl.ds(start, count)
        arrive.append(pltpu.make_async_copy(src.at[rows], buffer.at[rows], sem.at[0, k]))
        leave.append(pltpu.make_async_copy(buffer.at[rows], dst.at[rows], sem.at[1, k]))
        arrive[k].start()
    for k in range(len(pieces)):
        arrive[k].wait()
        leave[k].start()
    for copy in leave:
        copy.wait()


def call(comm, *args):
    (node, fine, coarse, fs, fr, co, cr, cv, ef, eb, e2, eg, nf, nb, n2, ng) = args
    anyspec = pl.BlockSpec(memory_space=pl.ANY)
    vmem = pl.BlockSpec(memory_space=pltpu.VMEM)
    copies = 5
    results = pl.pallas_call(
        functools.partial(kernel, comm=comm),
        name="processor",
        out_shape=(
            jax.ShapeDtypeStruct((NODE, D), BF16),
            jax.ShapeDtypeStruct((FINE, D), BF16),
            jax.ShapeDtypeStruct((CE, D), BF16),
        ),
        in_specs=[anyspec] * 3 + [vmem] * 5 + [anyspec, vmem, anyspec, vmem] * 2,
        out_specs=(anyspec, anyspec, anyspec),
        scratch_shapes=[
            pltpu.VMEM((FINE, D + TABLE), BF16),
            pltpu.VMEM((NODE, FINE), BF16),
            pltpu.VMEM((CE, D), BF16),
            pltpu.VMEM((CE, GATHERED), BF16),
            pltpu.VMEM((CE, 128), BF16),
            pltpu.VMEM((COARSE, CE), BF16),
            pltpu.VMEM((LAYERS, D + TABLE, D), BF16),
            pltpu.VMEM((LAYERS, 2 * D, D), BF16),
            pltpu.VMEM((LAYERS, D, D), BF16),
            pltpu.VMEM((LAYERS, 2 * D, D), BF16),
            pltpu.VMEM((LAYERS, D, D), BF16),
            pltpu.VMEM((LAYERS + 1, NODE, D), BF16),
            pltpu.VMEM((LAYERS, 2 * HALO, D), BF16),
            pltpu.VMEM((LAYERS, GATHERED, D), BF16),
            pltpu.VMEM((NODE, D), F32),
            pltpu.VMEM((CE, D), F32),
            pltpu.VMEM((NODE, D), F32),
            pltpu.SemaphoreType.DMA((9,)),
            pltpu.SemaphoreType.DMA((2 * CHUNKS,)),
            pltpu.SemaphoreType.DMA((6,)),
            pltpu.SemaphoreType.DMA((LAYERS, copies)),
            pltpu.SemaphoreType.DMA((LAYERS, copies)),
        ],
        compiler_params=pltpu.CompilerParams(
            collective_id=0 if comm else None, has_side_effects=True, vmem_limit_bytes=56 * 1024 * 1024
        ),
    )(
        node, fine, coarse,
        fs.reshape(FINE // 128, 128), fr.reshape(FINE // 128, 128),
        co.reshape(CE // 128, 128), cr.reshape(CE // 128, 128), cv.reshape(CE // 128, 128),
        ef, eb, e2, eg, nf, nb, n2, ng,
    )
    return pl.pallas_call(
        hand_over,
        name="hand_over",
        out_shape=tuple(jax.ShapeDtypeStruct((n, D), BF16) for n in (NODE, FINE, CE)),
        in_specs=[anyspec] * 3,
        out_specs=(anyspec,) * 3,
        scratch_shapes=[pltpu.VMEM((n, D), BF16) for n in (NODE, FINE, CE)] + [pltpu.SemaphoreType.DMA((2, 6))],
    )(*results)


def solution(mesh):
    rows = P(("group", "patch"), None)
    flat = P(("group", "patch"))
    in_specs = (rows, rows, rows, flat, flat, rows, flat, flat) + (P(),) * 8
    return jax.shard_map(
        functools.partial(call, True), mesh=mesh, in_specs=in_specs, out_specs=(rows, rows, rows), check_vma=False
    )
```

```python
import functools

import jax
import jax.numpy as jnp
from jax import lax
from jax.experimental import pallas as pl
from jax.experimental.pallas import tpu as pltpu
from jax.sharding import PartitionSpec as P

D = 512
NODE = 320
FINE = 2048
CE = 512
HALO = 64
COARSE = 16
LAYERS = 2
PAD = NODE + 2 * HALO
TABLE = PAD + NODE
GATHERED = 128 * COARSE
CHUNK = 512
CHUNKS = FINE // CHUNK
EPSILON = 1e-05
F32 = jnp.float32
BF16 = jnp.bfloat16


def mm(a, b):
    return jnp.dot(a, b, preferred_element_type=F32)


def silu_half(pre):
    u = (pre * 0.5).astype(BF16)
    return u + u * jnp.tanh(u)


def norm_rows(values, gain_row):
    centred = values - jnp.mean(values, axis=-1, keepdims=True)
    variance = jnp.mean(centred * centred, axis=-1, keepdims=True)
    return centred * lax.rsqrt(variance + EPSILON) * gain_row


def onehot(cond):
    return jnp.where(cond, 1.0, 0.0).astype(BF16)


def column(row):
    return jnp.transpose(jnp.broadcast_to(row, (128, 128)))


def kernel(
    h_hbm, fine_hbm, coarse_hbm, fs_hbm, fr_hbm, co_hbm, cr_hbm, cv_hbm,
    ef_hbm, eb_hbm, e2_hbm, eg_hbm, nf_hbm, nb_hbm, n2_hbm, ng_hbm,
    node_out, fine_out, coarse_out,
    L, ohT, CL, coh, crh, cohT, R, Wsr, W2, Nf, N2, H, halo, T, agg, pc, pn,
    fs, fr, co, cr, cv, eb, eg, nb, ng,
    lsem, fsem, osem, ssem, rsem,
    *, comm,
):
    plan = [
        ("fs", fs_hbm, fs),
        ("fr", fr_hbm, fr),
        ("h", h_hbm, H.at[0]),
        ("wsr0", ef_hbm.at[0, pl.ds(D, 2 * D)], Wsr.at[0]),
        ("eb", eb_hbm, eb),
        ("r0", ef_hbm.at[0, pl.ds(0, D)], R.at[0, pl.ds(0, D)]),
        ("w2", e2_hbm, W2),
        ("eg", eg_hbm, eg),
        ("co", co_hbm, co),
        ("cr", cr_hbm, cr),
        ("cv", cv_hbm, cv),
        ("nf", nf_hbm, Nf),
        ("nb", nb_hbm, nb),
        ("coarse", coarse_hbm, CL),
        ("n2", n2_hbm, N2),
        ("ng", ng_hbm, ng),
        ("wsr1", ef_hbm.at[1, pl.ds(D, 2 * D)], Wsr.at[1]),
        ("r1", ef_hbm.at[1, pl.ds(0, D)], R.at[1, pl.ds(0, D)]),
    ]
    loads = {name: pltpu.make_async_copy(src, dst, lsem.at[k]) for k, (name, src, dst) in enumerate(plan)}

    def fine_load(i):
        rows = pl.ds(pl.multiple_of(i * CHUNK, CHUNK), CHUNK)
        return pltpu.make_async_copy(fine_hbm.at[rows], L.at[rows, pl.ds(0, D)], fsem.at[i])

    def fine_store(i):
        rows = pl.ds(pl.multiple_of(i * CHUNK, CHUNK), CHUNK)
        return pltpu.make_async_copy(L.at[rows, pl.ds(0, D)], fine_out.at[rows], fsem.at[CHUNKS + i])

    def start_loads():
        for name, _, _ in plan[:6]:
            loads[name].start()
        fine_load(0).start()
        loads["w2"].start()
        loads["eg"].start()
        for i in range(1, CHUNKS):
            fine_load(i).start()
        for name, _, _ in plan[8:]:
            loads[name].start()

    if comm:
        group = lax.axis_index("group")
        patch = lax.axis_index("patch")
        z, c = group // 2, group % 2
        x, y = patch // 4, patch % 4
        here = (x, y, z)

        def swap1(i):
            return i + 1 - 2 * (i % 2)

        def swap3(i):
            return 3 - i

        def cube(swap, order):
            targets = []
            for mask in order:
                tx, ty, tz = (swap(i) if mask >> k & 1 else i for k, i in enumerate(here))
                targets.append({"group": tz * 2 + c, "patch": tx * 4 + ty})
            return targets

        swaps = (swap1, swap3)
        stages = ((4,), (6, 2), (7, 5, 3, 1))
        first = [[cube(swaps[side], masks) for masks in stages] for side in range(2)]
        second = [cube(swaps[1 - side], (7, 6, 5, 3, 4, 2, 1)) for side in range(2)]
        partner = {"group": z * 2 + (1 - c), "patch": patch}
        following = {"group": group, "patch": (patch + 1) % 16}
        previous = {"group": group, "patch": (patch + 15) % 16}

        def bundle(side):
            pair = [(i + side) // 2 % 2 for i in here]
            return ((c * 2 + side) * 8 + pair[0] * 4 + pair[1] * 2 + pair[2]) * 64

        wx, wy, wz = (i % 2 for i in here)
        within = (wx * 4 + wy * 2 + wz) * 8
        pieces = (
            ((wx * 4 + wy * 2) * 8, 16),
            ((wx * 4 + (1 - wy) * 2) * 8, 16),
            ((1 - wx) * 32, 32),
        )

        def remote(l, k, src, dst, target):
            return pltpu.make_async_remote_copy(
                src_ref=src, dst_ref=dst, send_sem=ssem.at[l, k], recv_sem=rsem.at[l, k],
                device_id=target, device_id_type=pl.DeviceIdType.MESH,
            )

        def same(l, k, start, count, target):
            ref = T.at[l, pl.ds(pl.multiple_of(start, 8), count)]
            return remote(l, k, ref, ref, target)

        def halos(l, source):
            return [
                remote(l, 0, source.at[pl.ds(NODE - HALO, HALO)], halo.at[l, pl.ds(0, HALO)], following),
                remote(l, 1, source.at[pl.ds(0, HALO)], halo.at[l, pl.ds(HALO, HALO)], previous),
            ]

        def own(l, side, source):
            dst = T.at[l, pl.ds(pl.multiple_of(bundle(side) + within, 8), 8)]
            return source.at[pl.ds(side * 8, 8)], dst

        def exchange(l):
            return same(l, 8, c * 1024, 1024, partner)

        barrier = pltpu.get_barrier_semaphore()
        peers = [*second[0], *second[1], partner, following, previous]
        for peer in peers:
            pl.semaphore_signal(barrier, inc=1, device_id=peer, device_id_type=pl.DeviceIdType.MESH)

        def begin(l, source):
            for k in range(3):
                for side in range(2):
                    for target in first[side][k]:
                        remote(l, 2 + k, *own(l, side, source), target).start()
            for side in range(2):
                pltpu.make_async_copy(*own(l, side, source), osem.at[2 + 2 * l + side]).start()
            for copy in halos(l, source):
                copy.start()

        def step1(l, k):
            same(l, 2 + k, 0, 2 * len(stages[k]) * 8, partner).wait_recv()
            if k == 0:
                for side in range(2):
                    pltpu.make_async_copy(*own(l, side, H.at[l]), osem.at[2 + 2 * l + side]).wait()
            start, count = pieces[k]
            for t in range(7):
                for side in range(2):
                    same(l, 5 + k, bundle(side) + start, count, second[side][t]).start()

        def step2(l):
            for k in range(3):
                same(l, 5 + k, 0, 14 * pieces[k][1], partner).wait_recv()
            exchange(l).start()

        def finish(l):
            exchange(l).wait_recv()

        def drain(l):
            for k in range(3):
                same(l, 2 + k, 0, 2 * len(stages[k]) * 8, partner).wait_send()
                same(l, 5 + k, 0, 14 * pieces[k][1], partner).wait_send()
            for copy in [*halos(l, H.at[l]), exchange(l)]:
                copy.wait_send()

        def wait_halos(l):
            for copy in halos(l, H.at[l]):
                copy.wait_recv()
    else:
        c = 0
        begin = step1 = step2 = finish = drain = wait_halos = lambda *a: None

    lane = lax.broadcasted_iota(jnp.int32, (128, 128), 1)
    row_node = lax.broadcasted_iota(jnp.int32, (NODE, 128), 0)

    def build_fine(k, carry):
        sender = column(fs[pl.ds(k, 1), :])
        receiver_row = fr[pl.ds(k, 1), :]
        receiver = column(receiver_row) + PAD
        rows = pl.ds(pl.multiple_of(k * 128, 128), 128)
        for b in range(TABLE // 128):
            at = lane + b * 128
            if b < 3:
                cond = sender == at
            elif b == 3:
                cond = (sender == at) | (receiver == at)
            else:
                cond = receiver == at
            L[rows, D + b * 128 : D + (b + 1) * 128] = onehot(cond)
        ohT[:, rows] = onehot(row_node == receiver_row)
        return carry

    def build_coarse(k, carry):
        owner = co[pl.ds(k, 1), :]
        row = cr[pl.ds(k, 1), :]
        oz, oc, ox, oy = owner >> 5, (owner >> 4) & 1, (owner >> 2) & 3, owner & 3
        side = row >> 3
        px, py, pz = (((i + side) >> 1) & 1 for i in (ox, oy, oz))
        place = ((px * 2 + py) * 2 + pz) * 8 + ((ox & 1) * 2 + (oy & 1)) * 2 + (oz & 1)
        sender = column(((oc * 2 + side) * 64 + place) * 8 + (row & 7))
        receiver_row = cv[pl.ds(k, 1), :]
        rows = pl.ds(pl.multiple_of(k * 128, 128), 128)
        for b in range(GATHERED // 128):
            coh[rows, b * 128 : (b + 1) * 128] = onehot(sender == lane + b * 128)
        crh[rows, :] = onehot(column(receiver_row) == lane)
        cohT[:, rows] = onehot(lax.broadcasted_iota(jnp.int32, (COARSE, 128), 0) == receiver_row)
        return carry

    start_loads()
    if comm:
        pl.semaphore_wait(barrier, len(peers))
    begin(0, h_hbm)
    for name in ("fs", "fr"):
        loads[name].wait()
    lax.fori_loop(0, FINE // 128, build_fine, 0)
    for name in ("h", "wsr0", "eb"):
        loads[name].wait()

    def fine_chunk(l, i):
        rows = pl.ds(pl.multiple_of(i * CHUNK, CHUNK), CHUNK)
        hidden = silu_half(mm(L[rows, :], R[l]))
        message = norm_rows(mm(hidden, W2[l]), eg[pl.ds(l, 1), :]).astype(BF16)
        L[rows, 0:D] += message
        agg[...] += mm(ohT[:, rows], message)

    def node_rows(l, start, count, received):
        rows = slice(start, start + count)
        hidden = silu_half(pn[rows] + mm(received.astype(BF16), Nf[l, D : 2 * D]))
        update = norm_rows(mm(hidden, N2[l]), ng[pl.ds(l, 1), :])
        H[l + 1, rows] = (H[l, rows].astype(F32) + update).astype(BF16)

    def layer(l, carry):
        latent = H[l]
        R[l, D + HALO : D + HALO + NODE] = mm(latent, Wsr[l, 0:D]).astype(BF16)
        R[l, D + PAD : D + TABLE] = (mm(latent, Wsr[l, D : 2 * D]) + eb[pl.ds(l, 1), :]).astype(BF16)
        agg[...] = jnp.zeros_like(agg)
        step1(l, 0)
        step1(l, 1)
        wait_halos(l)
        ends = mm(halo[l], Wsr[l, 0:D]).astype(BF16)
        R[l, D : D + HALO] = ends[0:HALO]
        R[l, D + HALO + NODE : D + PAD] = ends[HALO : 2 * HALO]
        step1(l, 2)

        @pl.when(l == 0)
        def _():
            for name in ("r0", "w2", "eg"):
                loads[name].wait()

        def chunk_step(i, inner):
            @pl.when(l == 0)
            def _():
                fine_load(i).wait()

            fine_chunk(l, i)

            @pl.when(l == LAYERS - 1)
            def _():
                fine_store(i).start()

            return inner

        lax.fori_loop(0, CHUNKS, chunk_step, 0)
        step2(l)

        @pl.when(l == 0)
        def _():
            for name in ("co", "cr", "cv", "nf", "nb", "coarse", "n2", "ng", "wsr1", "r1"):
                loads[name].wait()
            lax.fori_loop(0, CE // 128, build_coarse, 0)

        pc[...] = mm(CL[...], R[l, 0:D]) + mm(crh[...], R[l, D + PAD : D + PAD + 128])
        pn[...] = mm(latent, Nf[l, 0:D]) + nb[pl.ds(l, 1), :]
        node_rows(l, COARSE, NODE - COARSE, agg[COARSE:NODE])
        mine = pl.ds(pl.multiple_of(c * 1024, 1024), 1024)
        other = pl.ds(pl.multiple_of((1 - c) * 1024, 1024), 1024)
        sender = mm(coh[:, mine], T[l, mine])
        finish(l)
        sender = (sender + mm(coh[:, other], T[l, other])).astype(BF16)
        hidden = silu_half(pc[...] + mm(sender, Wsr[l, 0:D]))
        message = norm_rows(mm(hidden, W2[l]), eg[pl.ds(l, 1), :]).astype(BF16)
        node_rows(l, 0, COARSE, agg[0:COARSE] + mm(cohT[...], message))

        @pl.when(l < LAYERS - 1)
        def _():
            begin(l + 1, H.at[l + 1])

        CL[...] += message
        drain(l)
        return carry

    lax.fori_loop(0, LAYERS, layer, 0)
    finals = [
        pltpu.make_async_copy(CL, coarse_out, osem.at[0]),
        pltpu.make_async_copy(H.at[LAYERS], node_out, osem.at[1]),
    ]
    for copy in finals:
        copy.start()
    for i in range(CHUNKS):
        fine_store(i).wait()
    for copy in finals:
        copy.wait()


def hand_over(node, fine, coarse, node_out, fine_out, coarse_out, N, F, C, sem):
    pieces = [(coarse, C, coarse_out, 0, CE), (node, N, node_out, 0, NODE)]
    pieces += [(fine, F, fine_out, k * 512, 512) for k in range(FINE // 512)]
    arrive, leave = [], []
    for k, (src, buffer, dst, start, count) in enumerate(pieces):
        rows = pl.ds(start, count)
        arrive.append(pltpu.make_async_copy(src.at[rows], buffer.at[rows], sem.at[0, k]))
        leave.append(pltpu.make_async_copy(buffer.at[rows], dst.at[rows], sem.at[1, k]))
        arrive[k].start()
    for k in range(len(pieces)):
        arrive[k].wait()
        leave[k].start()
    for copy in leave:
        copy.wait()


def call(comm, *args):
    (node, fine, coarse, fs, fr, co, cr, cv, ef, eb, e2, eg, nf, nb, n2, ng) = args
    anyspec = pl.BlockSpec(memory_space=pl.ANY)
    copies = 9
    results = pl.pallas_call(
        functools.partial(kernel, comm=comm),
        name="processor",
        out_shape=(
            jax.ShapeDtypeStruct((NODE, D), BF16),
            jax.ShapeDtypeStruct((FINE, D), BF16),
            jax.ShapeDtypeStruct((CE, D), BF16),
        ),
        in_specs=[anyspec] * 16,
        out_specs=(anyspec, anyspec, anyspec),
        scratch_shapes=[
            pltpu.VMEM((FINE, D + TABLE), BF16),
            pltpu.VMEM((NODE, FINE), BF16),
            pltpu.VMEM((CE, D), BF16),
            pltpu.VMEM((CE, GATHERED), BF16),
            pltpu.VMEM((CE, 128), BF16),
            pltpu.VMEM((COARSE, CE), BF16),
            pltpu.VMEM((LAYERS, D + TABLE, D), BF16),
            pltpu.VMEM((LAYERS, 2 * D, D), BF16),
            pltpu.VMEM((LAYERS, D, D), BF16),
            pltpu.VMEM((LAYERS, 2 * D, D), BF16),
            pltpu.VMEM((LAYERS, D, D), BF16),
            pltpu.VMEM((LAYERS + 1, NODE, D), BF16),
            pltpu.VMEM((LAYERS, 2 * HALO, D), BF16),
            pltpu.VMEM((LAYERS, GATHERED, D), BF16),
            pltpu.VMEM((NODE, D), F32),
            pltpu.VMEM((CE, D), F32),
            pltpu.VMEM((NODE, D), F32),
            pltpu.VMEM((FINE // 128, 128), jnp.int32),
            pltpu.VMEM((FINE // 128, 128), jnp.int32),
            pltpu.VMEM((CE // 128, 128), jnp.int32),
            pltpu.VMEM((CE // 128, 128), jnp.int32),
            pltpu.VMEM((CE // 128, 128), jnp.int32),
            pltpu.VMEM((LAYERS, D), F32),
            pltpu.VMEM((LAYERS, D), F32),
            pltpu.VMEM((LAYERS, D), F32),
            pltpu.VMEM((LAYERS, D), F32),
            pltpu.SemaphoreType.DMA((18,)),
            pltpu.SemaphoreType.DMA((2 * CHUNKS,)),
            pltpu.SemaphoreType.DMA((6,)),
            pltpu.SemaphoreType.DMA((LAYERS, copies)),
            pltpu.SemaphoreType.DMA((LAYERS, copies)),
        ],
        compiler_params=pltpu.CompilerParams(
            collective_id=0 if comm else None, has_side_effects=True, vmem_limit_bytes=56 * 1024 * 1024
        ),
    )(
        node, fine, coarse,
        fs.reshape(FINE // 128, 128), fr.reshape(FINE // 128, 128),
        co.reshape(CE // 128, 128), cr.reshape(CE // 128, 128), cv.reshape(CE // 128, 128),
        ef, eb, e2, eg, nf, nb, n2, ng,
    )
    return pl.pallas_call(
        hand_over,
        name="hand_over",
        out_shape=tuple(jax.ShapeDtypeStruct((n, D), BF16) for n in (NODE, FINE, CE)),
        in_specs=[anyspec] * 3,
        out_specs=(anyspec,) * 3,
        scratch_shapes=[pltpu.VMEM((n, D), BF16) for n in (NODE, FINE, CE)] + [pltpu.SemaphoreType.DMA((2, 6))],
    )(*results)


def solution(mesh):
    rows = P(("group", "patch"), None)
    flat = P(("group", "patch"))
    in_specs = (rows, rows, rows, flat, flat, rows, flat, flat) + (P(),) * 8
    return jax.shard_map(
        functools.partial(call, True), mesh=mesh, in_specs=in_specs, out_specs=(rows, rows, rows), check_vma=False
    )
```

```python
import functools

import jax
import jax.numpy as jnp
from jax import lax
from jax.experimental import pallas as pl
from jax.experimental.pallas import tpu as pltpu
from jax.sharding import PartitionSpec as P

D = 512
NODE = 320
FINE = 2048
CE = 512
HALO = 64
COARSE = 16
LAYERS = 2
PAD = NODE + 2 * HALO
TABLE = PAD + NODE
GATHERED = 128 * COARSE
CHUNK = 2048
CHUNKS = FINE // CHUNK
COARSE_CHUNK = 512
EPSILON = 1e-05
F32 = jnp.float32
BF16 = jnp.bfloat16


def mm(a, b):
    return jnp.dot(a, b, preferred_element_type=F32)


def silu_half(pre):
    u = (pre * 0.5).astype(BF16)
    return u + u * jnp.tanh(u)


def norm_rows(values, gain_row):
    centred = values - jnp.mean(values, axis=-1, keepdims=True)
    variance = jnp.mean(centred * centred, axis=-1, keepdims=True)
    return centred * lax.rsqrt(variance + EPSILON) * gain_row


def onehot(cond):
    return jnp.where(cond, 1.0, 0.0).astype(BF16)


def column(row):
    return jnp.transpose(jnp.broadcast_to(row, (128, 128)))


def kernel(
    h_hbm, fine_hbm, coarse_hbm, fs_hbm, fr_hbm, co_hbm, cr_hbm, cv_hbm,
    ef_hbm, eb_hbm, e2_hbm, eg_hbm, nf_hbm, nb_hbm, n2_hbm, ng_hbm,
    node_out, fine_out, coarse_out,
    L, ohT, CL, coh, crh, cohT, R, Wsr, W2, Nf, N2, H, halo, T, agg, pc, ps, pn,
    fs, fr, co, cr, cv, eb, eg, nb, ng,
    lsem, fsem, osem, ssem, rsem,
    *, comm,
):
    plan = [
        ("fs", fs_hbm, fs),
        ("fr", fr_hbm, fr),
        ("h", h_hbm, H.at[0]),
        ("wsr0", ef_hbm.at[0, pl.ds(D, 2 * D)], Wsr.at[0]),
        ("eb", eb_hbm, eb),
        ("r0", ef_hbm.at[0, pl.ds(0, D)], R.at[0, pl.ds(0, D)]),
        ("w2", e2_hbm, W2),
        ("eg", eg_hbm, eg),
        ("co", co_hbm, co),
        ("cr", cr_hbm, cr),
        ("cv", cv_hbm, cv),
        ("nf", nf_hbm, Nf),
        ("nb", nb_hbm, nb),
        ("coarse", coarse_hbm, CL),
        ("n2", n2_hbm, N2),
        ("ng", ng_hbm, ng),
        ("wsr1", ef_hbm.at[1, pl.ds(D, 2 * D)], Wsr.at[1]),
        ("r1", ef_hbm.at[1, pl.ds(0, D)], R.at[1, pl.ds(0, D)]),
    ]
    loads = {name: pltpu.make_async_copy(src, dst, lsem.at[k]) for k, (name, src, dst) in enumerate(plan)}

    def fine_load(i):
        rows = pl.ds(pl.multiple_of(i * CHUNK, CHUNK), CHUNK)
        return pltpu.make_async_copy(fine_hbm.at[rows], L.at[rows, pl.ds(0, D)], fsem.at[i])

    def start_loads():
        for name, _, _ in [*plan[:6], *plan[8:11]]:
            loads[name].start()
        fine_load(0).start()
        loads["w2"].start()
        loads["eg"].start()
        for i in range(1, CHUNKS):
            fine_load(i).start()
        for name, _, _ in plan[11:]:
            loads[name].start()

    if comm:
        group = lax.axis_index("group")
        patch = lax.axis_index("patch")
        z, c = group // 2, group % 2
        x, y = patch // 4, patch % 4
        here = (x, y, z)

        def swap1(i):
            return i + 1 - 2 * (i % 2)

        def swap3(i):
            return 3 - i

        def cube(swap, order):
            targets = []
            for mask in order:
                tx, ty, tz = (swap(i) if mask >> k & 1 else i for k, i in enumerate(here))
                targets.append({"group": tz * 2 + c, "patch": tx * 4 + ty})
            return targets

        swaps = (swap1, swap3)
        stages = ((4,), (6, 2), (7, 5, 3, 1))
        first = [[cube(swaps[side], masks) for masks in stages] for side in range(2)]
        second = [cube(swaps[1 - side], (7, 6, 5, 3, 4, 2, 1)) for side in range(2)]
        partner = {"group": z * 2 + (1 - c), "patch": patch}
        following = {"group": group, "patch": (patch + 1) % 16}
        previous = {"group": group, "patch": (patch + 15) % 16}

        def bundle(side):
            pair = [(i + side) // 2 % 2 for i in here]
            return ((c * 2 + side) * 8 + pair[0] * 4 + pair[1] * 2 + pair[2]) * 64

        wx, wy, wz = (i % 2 for i in here)
        within = (wx * 4 + wy * 2 + wz) * 8
        pieces = (
            ((wx * 4 + wy * 2) * 8, 16),
            ((wx * 4 + (1 - wy) * 2) * 8, 16),
            ((1 - wx) * 32, 32),
        )

        def remote(l, k, src, dst, target):
            return pltpu.make_async_remote_copy(
                src_ref=src, dst_ref=dst, send_sem=ssem.at[l, k], recv_sem=rsem.at[l, k],
                device_id=target, device_id_type=pl.DeviceIdType.MESH,
            )

        def same(l, k, start, count, target):
            ref = T.at[l, pl.ds(pl.multiple_of(start, 8), count)]
            return remote(l, k, ref, ref, target)

        def halos(l, source):
            return [
                remote(l, 0, source.at[pl.ds(NODE - HALO, HALO)], halo.at[l, pl.ds(0, HALO)], following),
                remote(l, 1, source.at[pl.ds(0, HALO)], halo.at[l, pl.ds(HALO, HALO)], previous),
            ]

        def own(l, side, source):
            dst = T.at[l, pl.ds(pl.multiple_of(bundle(side) + within, 8), 8)]
            return source.at[pl.ds(side * 8, 8)], dst

        def exchange(l):
            return same(l, 8, c * 1024, 1024, partner)

        barrier = pltpu.get_barrier_semaphore()
        peers = [*second[0], *second[1], partner, following, previous]
        for peer in peers:
            pl.semaphore_signal(barrier, inc=1, device_id=peer, device_id_type=pl.DeviceIdType.MESH)

        def begin(l, source):
            for k in range(3):
                for side in range(2):
                    for target in first[side][k]:
                        remote(l, 2 + k, *own(l, side, source), target).start()
            for side in range(2):
                pltpu.make_async_copy(*own(l, side, source), osem.at[2 + 2 * l + side]).start()
            for copy in halos(l, source):
                copy.start()

        def step1(l, k):
            same(l, 2 + k, 0, 2 * len(stages[k]) * 8, partner).wait_recv()
            if k == 0:
                for side in range(2):
                    pltpu.make_async_copy(*own(l, side, H.at[l]), osem.at[2 + 2 * l + side]).wait()
            start, count = pieces[k]
            for t in range(7):
                for side in range(2):
                    same(l, 5 + k, bundle(side) + start, count, second[side][t]).start()

        def step2(l):
            for k in range(3):
                same(l, 5 + k, 0, 14 * pieces[k][1], partner).wait_recv()
            exchange(l).start()

        def finish(l):
            exchange(l).wait_recv()

        def drain(l):
            for k in range(3):
                same(l, 2 + k, 0, 2 * len(stages[k]) * 8, partner).wait_send()
                same(l, 5 + k, 0, 14 * pieces[k][1], partner).wait_send()
            for copy in [*halos(l, H.at[l]), exchange(l)]:
                copy.wait_send()

        def wait_halos(l):
            for copy in halos(l, H.at[l]):
                copy.wait_recv()
    else:
        c = 0
        begin = step1 = step2 = finish = drain = wait_halos = lambda *a: None

    lane = lax.broadcasted_iota(jnp.int32, (128, 128), 1)
    row_node = lax.broadcasted_iota(jnp.int32, (NODE, 128), 0)

    def build_fine(k, carry):
        sender = column(fs[pl.ds(k, 1), :])
        receiver_row = fr[pl.ds(k, 1), :]
        receiver = column(receiver_row) + PAD
        rows = pl.ds(pl.multiple_of(k * 128, 128), 128)
        for b in range(TABLE // 128):
            at = lane + b * 128
            if b < 3:
                cond = sender == at
            elif b == 3:
                cond = (sender == at) | (receiver == at)
            else:
                cond = receiver == at
            L[rows, D + b * 128 : D + (b + 1) * 128] = onehot(cond)
        ohT[:, rows] = onehot(row_node == receiver_row)
        return carry

    def build_coarse(k, carry):
        owner = co[pl.ds(k, 1), :]
        row = cr[pl.ds(k, 1), :]
        oz, oc, ox, oy = owner >> 5, (owner >> 4) & 1, (owner >> 2) & 3, owner & 3
        side = row >> 3
        px, py, pz = (((i + side) >> 1) & 1 for i in (ox, oy, oz))
        place = ((px * 2 + py) * 2 + pz) * 8 + ((ox & 1) * 2 + (oy & 1)) * 2 + (oz & 1)
        sender = column(((oc * 2 + side) * 64 + place) * 8 + (row & 7))
        receiver_row = cv[pl.ds(k, 1), :]
        rows = pl.ds(pl.multiple_of(k * 128, 128), 128)
        for b in range(GATHERED // 128):
            coh[rows, b * 128 : (b + 1) * 128] = onehot(sender == lane + b * 128)
        crh[rows, :] = onehot(column(receiver_row) == lane)
        cohT[:, rows] = onehot(lax.broadcasted_iota(jnp.int32, (COARSE, 128), 0) == receiver_row)
        return carry

    start_loads()
    if comm:
        pl.semaphore_wait(barrier, len(peers))
    begin(0, h_hbm)
    for name in ("fs", "fr"):
        loads[name].wait()
    lax.fori_loop(0, FINE // 128, build_fine, 0)
    for name in ("h", "wsr0", "eb"):
        loads[name].wait()

    def fine_chunk(l, i):
        rows = pl.ds(pl.multiple_of(i * CHUNK, CHUNK), CHUNK)
        hidden = silu_half(mm(L[rows, :], R[l]))
        message = norm_rows(mm(hidden, W2[l]), eg[pl.ds(l, 1), :]).astype(BF16)
        L[rows, 0:D] += message
        agg[...] += mm(ohT[:, rows], message)

    def node_rows(l, start, count, received):
        rows = slice(start, start + count)
        hidden = silu_half(pn[rows] + mm(received.astype(BF16), Nf[l, D : 2 * D]))
        update = norm_rows(mm(hidden, N2[l]), ng[pl.ds(l, 1), :])
        H[l + 1, rows] = (H[l, rows].astype(F32) + update).astype(BF16)

    def layer(l, carry):
        latent = H[l]
        R[l, D + HALO : D + HALO + NODE] = mm(latent, Wsr[l, 0:D]).astype(BF16)
        R[l, D + PAD : D + TABLE] = (mm(latent, Wsr[l, D : 2 * D]) + eb[pl.ds(l, 1), :]).astype(BF16)
        agg[...] = jnp.zeros_like(agg)
        step1(l, 0)

        @pl.when(l == 0)
        def _():
            for name in ("co", "cr", "cv"):
                loads[name].wait()
            lax.fori_loop(0, CE // 128, build_coarse, 0)

        step1(l, 1)
        wait_halos(l)
        ends = mm(halo[l], Wsr[l, 0:D]).astype(BF16)
        R[l, D : D + HALO] = ends[0:HALO]
        R[l, D + HALO + NODE : D + PAD] = ends[HALO : 2 * HALO]
        step1(l, 2)

        @pl.when(l == 0)
        def _():
            for name in ("r0", "w2", "eg"):
                loads[name].wait()

        def chunk_step(i, inner):
            @pl.when(l == 0)
            def _():
                fine_load(i).wait()

            fine_chunk(l, i)

            @pl.when(l == LAYERS - 1)
            def _():
                rows = pl.ds(pl.multiple_of(i * CHUNK, CHUNK), CHUNK)
                fine_out[rows, :] = L[rows, 0:D]

            return inner

        lax.fori_loop(0, CHUNKS, chunk_step, 0)
        step2(l)

        @pl.when(l == 0)
        def _():
            for name in ("nf", "nb", "coarse", "n2", "ng", "wsr1", "r1"):
                loads[name].wait()

        pc[...] = mm(CL[...], R[l, 0:D]) + mm(crh[...], R[l, D + PAD : D + PAD + 128])
        pn[...] = mm(latent, Nf[l, 0:D]) + nb[pl.ds(l, 1), :]
        node_rows(l, COARSE, NODE - COARSE, agg[COARSE:NODE])
        mine = pl.ds(pl.multiple_of(c * 1024, 1024), 1024)
        other = pl.ds(pl.multiple_of((1 - c) * 1024, 1024), 1024)

        def first_half(k, inner):
            rows = pl.ds(pl.multiple_of(k * 256, 256), 256)
            ps[rows, :] = mm(coh[rows, mine], T[l, mine])
            return inner

        lax.fori_loop(0, CE // 256, first_half, 0)
        finish(l)
        received = agg[0:COARSE]
        messages = []
        for start in range(0, CE, COARSE_CHUNK):
            rows = slice(start, start + COARSE_CHUNK)
            sender = (ps[rows] + mm(coh[rows, other], T[l, other])).astype(BF16)
            hidden = silu_half(pc[rows] + mm(sender, Wsr[l, 0:D]))
            message = norm_rows(mm(hidden, W2[l]), eg[pl.ds(l, 1), :]).astype(BF16)
            received = received + mm(cohT[:, rows], message)
            messages.append(message)
        node_rows(l, 0, COARSE, received)

        @pl.when(l < LAYERS - 1)
        def _():
            begin(l + 1, H.at[l + 1])

        for k, message in enumerate(messages):
            CL[k * COARSE_CHUNK : (k + 1) * COARSE_CHUNK] += message
        drain(l)
        return carry

    lax.fori_loop(0, LAYERS, layer, 0)
    node_out[...] = H[LAYERS]
    coarse_out[...] = CL[...]


def hand_over(node, fine, coarse, node_out, fine_out, coarse_out, sem):
    copies = [
        pltpu.make_async_copy(src, dst, sem.at[k])
        for k, (src, dst) in enumerate(((fine, fine_out), (coarse, coarse_out), (node, node_out)))
    ]
    for copy in copies:
        copy.start()
    for copy in copies:
        copy.wait()


def call(comm, *args):
    (node, fine, coarse, fs, fr, co, cr, cv, ef, eb, e2, eg, nf, nb, n2, ng) = args
    hbm = pl.BlockSpec(memory_space=pltpu.HBM)
    vmem = pl.BlockSpec(memory_space=pltpu.VMEM)
    copies = 9
    results = pl.pallas_call(
        functools.partial(kernel, comm=comm),
        name="processor",
        out_shape=tuple(pltpu.VMEM((n, D), BF16) for n in (NODE, FINE, CE)),
        in_specs=[hbm] * 16,
        out_specs=(vmem,) * 3,
        scratch_shapes=[
            pltpu.VMEM((FINE, D + TABLE), BF16),
            pltpu.VMEM((NODE, FINE), BF16),
            pltpu.VMEM((CE, D), BF16),
            pltpu.VMEM((CE, GATHERED), BF16),
            pltpu.VMEM((CE, 128), BF16),
            pltpu.VMEM((COARSE, CE), BF16),
            pltpu.VMEM((LAYERS, D + TABLE, D), BF16),
            pltpu.VMEM((LAYERS, 2 * D, D), BF16),
            pltpu.VMEM((LAYERS, D, D), BF16),
            pltpu.VMEM((LAYERS, 2 * D, D), BF16),
            pltpu.VMEM((LAYERS, D, D), BF16),
            pltpu.VMEM((LAYERS + 1, NODE, D), BF16),
            pltpu.VMEM((LAYERS, 2 * HALO, D), BF16),
            pltpu.VMEM((LAYERS, GATHERED, D), BF16),
            pltpu.VMEM((NODE, D), F32),
            pltpu.VMEM((CE, D), F32),
            pltpu.VMEM((CE, D), F32),
            pltpu.VMEM((NODE, D), F32),
            pltpu.VMEM((FINE // 128, 128), jnp.int32),
            pltpu.VMEM((FINE // 128, 128), jnp.int32),
            pltpu.VMEM((CE // 128, 128), jnp.int32),
            pltpu.VMEM((CE // 128, 128), jnp.int32),
            pltpu.VMEM((CE // 128, 128), jnp.int32),
            pltpu.VMEM((LAYERS, D), F32),
            pltpu.VMEM((LAYERS, D), F32),
            pltpu.VMEM((LAYERS, D), F32),
            pltpu.VMEM((LAYERS, D), F32),
            pltpu.SemaphoreType.DMA((18,)),
            pltpu.SemaphoreType.DMA((CHUNKS,)),
            pltpu.SemaphoreType.DMA((6,)),
            pltpu.SemaphoreType.DMA((LAYERS, copies)),
            pltpu.SemaphoreType.DMA((LAYERS, copies)),
        ],
        compiler_params=pltpu.CompilerParams(
            collective_id=0 if comm else None, has_side_effects=True, vmem_limit_bytes=56 * 1024 * 1024
        ),
    )(
        node, fine, coarse,
        fs.reshape(FINE // 128, 128), fr.reshape(FINE // 128, 128),
        co.reshape(CE // 128, 128), cr.reshape(CE // 128, 128), cv.reshape(CE // 128, 128),
        ef, eb, e2, eg, nf, nb, n2, ng,
    )
    anywhere = pl.BlockSpec(memory_space=pl.ANY)
    return pl.pallas_call(
        hand_over,
        name="hand_over",
        out_shape=tuple(jax.ShapeDtypeStruct((n, D), BF16) for n in (NODE, FINE, CE)),
        in_specs=[anywhere] * 3,
        out_specs=(hbm,) * 3,
        scratch_shapes=[pltpu.SemaphoreType.DMA((3,))],
        compiler_params=pltpu.CompilerParams(vmem_limit_bytes=1024 * 1024),
    )(*results)

def solution(mesh):
    rows = P(("group", "patch"), None)
    flat = P(("group", "patch"))
    in_specs = (rows, rows, rows, flat, flat, rows, flat, flat) + (P(),) * 8
    return jax.shard_map(
        functools.partial(call, True), mesh=mesh, in_specs=in_specs, out_specs=(rows, rows, rows), check_vma=False
    )
```

```python
import functools

import jax
import jax.numpy as jnp
from jax import lax
from jax.experimental import pallas as pl
from jax.experimental.pallas import tpu as pltpu
from jax.sharding import PartitionSpec as P

D = 512
NODE = 320
FINE = 2048
CE = 512
HALO = 64
COARSE = 16
LAYERS = 2
PAD = NODE + 2 * HALO
TABLE = PAD + NODE
GATHERED = 128 * COARSE
CHUNK = 2048
CHUNKS = FINE // CHUNK
COARSE_CHUNK = 512
EPSILON = 1e-05
F32 = jnp.float32
BF16 = jnp.bfloat16


def mm(a, b):
    return jnp.dot(a, b, preferred_element_type=F32)


def silu_half(pre):
    u = (pre * 0.5).astype(BF16)
    return u + u * jnp.tanh(u)


def centre(ref, l):
    weights = ref[l].astype(F32)
    ref[l] = (weights - jnp.mean(weights, axis=-1, keepdims=True)).astype(BF16)


def norm_rows(centred, gain_row):
    variance = jnp.mean(centred * centred, axis=-1, keepdims=True)
    return centred * lax.rsqrt(variance + EPSILON) * gain_row


def onehot(cond):
    return jnp.where(cond, 1.0, 0.0).astype(BF16)


def column(row):
    return jnp.transpose(jnp.broadcast_to(row, (128, 128)))


def kernel(
    h_hbm, fine_hbm, coarse_hbm, fs_hbm, fr_hbm, co_hbm, cr_hbm, cv_hbm,
    ef_hbm, eb_hbm, e2_hbm, eg_hbm, nf_hbm, nb_hbm, n2_hbm, ng_hbm,
    node_out, fine_out, coarse_out,
    L, ohT, CL, coh, crh, cohT, R, Wsr, W2, Nf, N2, H, halo, T, agg, pc, ps, pn,
    fs, fr, co, cr, cv, eb, eg, nb, ng,
    lsem, fsem, osem, ssem, rsem,
    *, comm,
):
    plan = [
        ("fs", fs_hbm, fs),
        ("fr", fr_hbm, fr),
        ("h", h_hbm, H.at[0]),
        ("wsr0", ef_hbm.at[0, pl.ds(D, 2 * D)], Wsr.at[0]),
        ("eb", eb_hbm, eb),
        ("r0", ef_hbm.at[0, pl.ds(0, D)], R.at[0, pl.ds(0, D)]),
        ("w2", e2_hbm, W2),
        ("eg", eg_hbm, eg),
        ("co", co_hbm, co),
        ("cr", cr_hbm, cr),
        ("cv", cv_hbm, cv),
        ("nf", nf_hbm, Nf),
        ("nb", nb_hbm, nb),
        ("coarse", coarse_hbm, CL),
        ("n2", n2_hbm, N2),
        ("ng", ng_hbm, ng),
        ("wsr1", ef_hbm.at[1, pl.ds(D, 2 * D)], Wsr.at[1]),
        ("r1", ef_hbm.at[1, pl.ds(0, D)], R.at[1, pl.ds(0, D)]),
    ]
    loads = {name: pltpu.make_async_copy(src, dst, lsem.at[k]) for k, (name, src, dst) in enumerate(plan)}

    def fine_load(i):
        rows = pl.ds(pl.multiple_of(i * CHUNK, CHUNK), CHUNK)
        return pltpu.make_async_copy(fine_hbm.at[rows], L.at[rows, pl.ds(0, D)], fsem.at[i])

    def start_loads():
        for name in ("fs", "fr", "h", "wsr0", "eb", "r0", "co", "cr", "cv", "coarse", "nf", "nb", "w2", "eg"):
            loads[name].start()
        for i in range(CHUNKS):
            fine_load(i).start()
        for name in ("n2", "ng", "wsr1", "r1"):
            loads[name].start()

    if comm:
        group = lax.axis_index("group")
        patch = lax.axis_index("patch")
        z, c = group // 2, group % 2
        x, y = patch // 4, patch % 4
        here = (x, y, z)

        def swap1(i):
            return i + 1 - 2 * (i % 2)

        def swap3(i):
            return 3 - i

        def cube(swap, order):
            targets = []
            for mask in order:
                tx, ty, tz = (swap(i) if mask >> k & 1 else i for k, i in enumerate(here))
                targets.append({"group": tz * 2 + c, "patch": tx * 4 + ty})
            return targets

        swaps = (swap1, swap3)
        stages = ((4,), (6, 2), (7, 5, 3, 1))
        first = [[cube(swaps[side], masks) for masks in stages] for side in range(2)]
        second = [cube(swaps[1 - side], (7, 6, 5, 3, 4, 2, 1)) for side in range(2)]
        partner = {"group": z * 2 + (1 - c), "patch": patch}
        following = {"group": group, "patch": (patch + 1) % 16}
        previous = {"group": group, "patch": (patch + 15) % 16}

        def bundle(side):
            pair = [(i + side) // 2 % 2 for i in here]
            return ((c * 2 + side) * 8 + pair[0] * 4 + pair[1] * 2 + pair[2]) * 64

        wx, wy, wz = (i % 2 for i in here)
        within = (wx * 4 + wy * 2 + wz) * 8
        pieces = (
            ((wx * 4 + wy * 2) * 8, 16),
            ((wx * 4 + (1 - wy) * 2) * 8, 16),
            ((1 - wx) * 32, 32),
        )

        def remote(l, k, src, dst, target):
            return pltpu.make_async_remote_copy(
                src_ref=src, dst_ref=dst, send_sem=ssem.at[l, (0, 1, 2, 2, 2, 2, 3)[k]], recv_sem=rsem.at[l, k],
                device_id=target, device_id_type=pl.DeviceIdType.MESH,
            )

        def same(l, k, start, count, target):
            ref = T.at[l, pl.ds(pl.multiple_of(start, 8), count)]
            return remote(l, k, ref, ref, target)

        def halos(l, source):
            return [
                remote(l, 0, source.at[pl.ds(NODE - HALO, HALO)], halo.at[l, pl.ds(0, HALO)], following),
                remote(l, 1, source.at[pl.ds(0, HALO)], halo.at[l, pl.ds(HALO, HALO)], previous),
            ]

        def own(l, side, source):
            dst = T.at[l, pl.ds(pl.multiple_of(bundle(side) + within, 8), 8)]
            return source.at[pl.ds(side * 8, 8)], dst

        def exchange(l):
            return same(l, 6, c * 1024, 1024, partner)

        barrier = pltpu.get_barrier_semaphore()
        peers = [*second[0], *second[1], partner, following, previous]
        for peer in peers:
            pl.semaphore_signal(barrier, inc=1, device_id=peer, device_id_type=pl.DeviceIdType.MESH)

        def begin(l, source):
            for k in range(3):
                for side in range(2):
                    for target in first[side][k]:
                        remote(l, 2 + k, *own(l, side, source), target).start()
            for side in range(2):
                pltpu.make_async_copy(*own(l, side, source), osem.at[l]).start()
            for copy in halos(l, source):
                copy.start()

        def step1(l, k):
            same(l, 2 + k, 0, 2 * len(stages[k]) * 8, partner).wait_recv()
            if k == 0:
                pltpu.make_async_copy(H.at[l, pl.ds(0, COARSE)], T.at[l, pl.ds(0, COARSE)], osem.at[l]).wait()
            start, count = pieces[k]
            for t in range(7):
                for side in range(2):
                    same(l, 5, bundle(side) + start, count, second[side][t]).start()

        def step2(l):
            same(l, 5, 0, 14 * 64, partner).wait_recv()
            exchange(l).start()

        def finish(l):
            exchange(l).wait_recv()

        def drain(l):
            same(l, 2, 0, 14 * 8 + 14 * 64, partner).wait_send()
            for copy in [*halos(l, H.at[l]), exchange(l)]:
                copy.wait_send()

        def wait_halos(l):
            for copy in halos(l, H.at[l]):
                copy.wait_recv()
    else:
        c = 0
        begin = step1 = step2 = finish = drain = wait_halos = lambda *a: None

    lane = lax.broadcasted_iota(jnp.int32, (128, 128), 1)
    row_node = lax.broadcasted_iota(jnp.int32, (NODE, 128), 0)

    def build_fine(k, carry):
        sender = column(fs[pl.ds(k, 1), :])
        receiver_row = fr[pl.ds(k, 1), :]
        receiver = column(receiver_row) + PAD
        rows = pl.ds(pl.multiple_of(k * 128, 128), 128)
        for b in range(TABLE // 128):
            at = lane + b * 128
            if b < 3:
                cond = sender == at
            elif b == 3:
                cond = (sender == at) | (receiver == at)
            else:
                cond = receiver == at
            L[rows, D + b * 128 : D + (b + 1) * 128] = onehot(cond)
        ohT[:, rows] = onehot(row_node == receiver_row)
        return carry

    def build_coarse(k, carry):
        owner = co[pl.ds(k, 1), :]
        row = cr[pl.ds(k, 1), :]
        oz, oc, ox, oy = owner >> 5, (owner >> 4) & 1, (owner >> 2) & 3, owner & 3
        side = row >> 3
        px, py, pz = (((i + side) >> 1) & 1 for i in (ox, oy, oz))
        place = ((px * 2 + py) * 2 + pz) * 8 + ((ox & 1) * 2 + (oy & 1)) * 2 + (oz & 1)
        sender = column(((oc * 2 + side) * 64 + place) * 8 + (row & 7))
        receiver_row = cv[pl.ds(k, 1), :]
        rows = pl.ds(pl.multiple_of(k * 128, 128), 128)
        for b in range(GATHERED // 128):
            coh[rows, b * 128 : (b + 1) * 128] = onehot(sender == lane + b * 128)
        crh[rows, :] = onehot(column(receiver_row) == lane)
        cohT[:, rows] = onehot(lax.broadcasted_iota(jnp.int32, (COARSE, 128), 0) == receiver_row)
        return carry

    if comm:
        pl.semaphore_wait(barrier, len(peers))
    begin(0, h_hbm)
    start_loads()
    for name in ("fs", "fr"):
        loads[name].wait()
    lax.fori_loop(0, FINE // 128, build_fine, 0)
    for name in ("h", "wsr0", "eb"):
        loads[name].wait()

    def fine_chunk(l, i):
        rows = pl.ds(pl.multiple_of(i * CHUNK, CHUNK), CHUNK)
        hidden = silu_half(mm(L[rows, :], R[l]))
        message = norm_rows(mm(hidden, W2[l]), eg[pl.ds(l, 1), :]).astype(BF16)
        L[rows, 0:D] += message
        agg[...] += mm(ohT[:, rows], message)

    def node_rows(l, start, count, received):
        rows = slice(start, start + count)
        hidden = silu_half(pn[rows] + mm(received.astype(BF16), Nf[l, D : 2 * D]))
        update = norm_rows(mm(hidden, N2[l]), ng[pl.ds(l, 1), :])
        H[l + 1, rows] = (H[l, rows].astype(F32) + update).astype(BF16)

    def layer(l, carry):
        latent = H[l]
        R[l, D + HALO : D + HALO + NODE] = mm(latent, Wsr[l, 0:D]).astype(BF16)
        R[l, D + PAD : D + TABLE] = (mm(latent, Wsr[l, D : 2 * D]) + eb[pl.ds(l, 1), :]).astype(BF16)
        agg[...] = jnp.zeros_like(agg)
        step1(l, 0)

        @pl.when(l == 0)
        def _():
            for name in ("r0", "co", "cr", "cv", "coarse", "nf", "nb"):
                loads[name].wait()
            lax.fori_loop(0, CE // 128, build_coarse, 0)

        pc[...] = mm(CL[...], R[l, 0:D]) + mm(crh[...], R[l, D + PAD : D + PAD + 128])
        pn[...] = mm(latent, Nf[l, 0:D]) + nb[pl.ds(l, 1), :]
        step1(l, 1)
        wait_halos(l)
        ends = mm(halo[l], Wsr[l, 0:D]).astype(BF16)
        R[l, D : D + HALO] = ends[0:HALO]
        R[l, D + HALO + NODE : D + PAD] = ends[HALO : 2 * HALO]
        step1(l, 2)

        @pl.when(l == 0)
        def _():
            for name in ("w2", "eg"):
                loads[name].wait()

        centre(W2, l)

        def chunk_step(i, inner):
            @pl.when(l == 0)
            def _():
                fine_load(i).wait()

            fine_chunk(l, i)

            @pl.when(l == LAYERS - 1)
            def _():
                rows = pl.ds(pl.multiple_of(i * CHUNK, CHUNK), CHUNK)
                fine_out[rows, :] = L[rows, 0:D]

            return inner

        lax.fori_loop(0, CHUNKS, chunk_step, 0)

        @pl.when(l == 0)
        def _():
            for name in ("n2", "ng", "wsr1", "r1"):
                loads[name].wait()

        centre(N2, l)
        node_rows(l, COARSE, NODE - COARSE, agg[COARSE:NODE])
        step2(l)
        mine = pl.ds(pl.multiple_of(c * 1024, 1024), 1024)
        other = pl.ds(pl.multiple_of((1 - c) * 1024, 1024), 1024)

        def first_half(k, inner):
            rows = pl.ds(pl.multiple_of(k * 256, 256), 256)
            ps[rows, :] = mm(coh[rows, mine], T[l, mine])
            return inner

        lax.fori_loop(0, CE // 256, first_half, 0)
        finish(l)
        received = agg[0:COARSE]
        messages = []
        for start in range(0, CE, COARSE_CHUNK):
            rows = slice(start, start + COARSE_CHUNK)
            sender = (ps[rows] + mm(coh[rows, other], T[l, other])).astype(BF16)
            hidden = silu_half(pc[rows] + mm(sender, Wsr[l, 0:D]))
            message = norm_rows(mm(hidden, W2[l]), eg[pl.ds(l, 1), :]).astype(BF16)
            received = received + mm(cohT[:, rows], message)
            messages.append(message)
        node_rows(l, 0, COARSE, received)

        @pl.when(l < LAYERS - 1)
        def _():
            begin(l + 1, H.at[l + 1])

        for k, message in enumerate(messages):
            CL[k * COARSE_CHUNK : (k + 1) * COARSE_CHUNK] += message
        drain(l)
        return carry

    lax.fori_loop(0, LAYERS, layer, 0)
    node_out[...] = H[LAYERS]
    coarse_out[...] = CL[...]


def hand_over(node, fine, coarse, node_out, fine_out, coarse_out, sem):
    copies = [
        pltpu.make_async_copy(src, dst, sem.at[k])
        for k, (src, dst) in enumerate(((fine, fine_out), (coarse, coarse_out), (node, node_out)))
    ]
    for copy in copies:
        copy.start()
    for copy in copies:
        copy.wait()


def call(comm, *args):
    (node, fine, coarse, fs, fr, co, cr, cv, ef, eb, e2, eg, nf, nb, n2, ng) = args
    hbm = pl.BlockSpec(memory_space=pltpu.HBM)
    vmem = pl.BlockSpec(memory_space=pltpu.VMEM)
    results = pl.pallas_call(
        functools.partial(kernel, comm=comm),
        name="processor",
        out_shape=tuple(pltpu.VMEM((n, D), BF16) for n in (NODE, FINE, CE)),
        in_specs=[hbm] * 16,
        out_specs=(vmem,) * 3,
        scratch_shapes=[
            pltpu.VMEM((FINE, D + TABLE), BF16),
            pltpu.VMEM((NODE, FINE), BF16),
            pltpu.VMEM((CE, D), BF16),
            pltpu.VMEM((CE, GATHERED), BF16),
            pltpu.VMEM((CE, 128), BF16),
            pltpu.VMEM((COARSE, CE), BF16),
            pltpu.VMEM((LAYERS, D + TABLE, D), BF16),
            pltpu.VMEM((LAYERS, 2 * D, D), BF16),
            pltpu.VMEM((LAYERS, D, D), BF16),
            pltpu.VMEM((LAYERS, 2 * D, D), BF16),
            pltpu.VMEM((LAYERS, D, D), BF16),
            pltpu.VMEM((LAYERS + 1, NODE, D), BF16),
            pltpu.VMEM((LAYERS, 2 * HALO, D), BF16),
            pltpu.VMEM((LAYERS, GATHERED, D), BF16),
            pltpu.VMEM((NODE, D), F32),
            pltpu.VMEM((CE, D), F32),
            pltpu.VMEM((CE, D), F32),
            pltpu.VMEM((NODE, D), F32),
            pltpu.VMEM((FINE // 128, 128), jnp.int32),
            pltpu.VMEM((FINE // 128, 128), jnp.int32),
            pltpu.VMEM((CE // 128, 128), jnp.int32),
            pltpu.VMEM((CE // 128, 128), jnp.int32),
            pltpu.VMEM((CE // 128, 128), jnp.int32),
            pltpu.VMEM((LAYERS, D), F32),
            pltpu.VMEM((LAYERS, D), F32),
            pltpu.VMEM((LAYERS, D), F32),
            pltpu.VMEM((LAYERS, D), F32),
            pltpu.SemaphoreType.DMA((18,)),
            pltpu.SemaphoreType.DMA((CHUNKS,)),
            pltpu.SemaphoreType.DMA((LAYERS,)),
            pltpu.SemaphoreType.DMA((LAYERS, 4)),
            pltpu.SemaphoreType.DMA((LAYERS, 7)),
        ],
        compiler_params=pltpu.CompilerParams(
            collective_id=0 if comm else None, has_side_effects=True, vmem_limit_bytes=56 * 1024 * 1024
        ),
    )(
        node, fine, coarse,
        fs.reshape(FINE // 128, 128), fr.reshape(FINE // 128, 128),
        co.reshape(CE // 128, 128), cr.reshape(CE // 128, 128), cv.reshape(CE // 128, 128),
        ef, eb, e2, eg, nf, nb, n2, ng,
    )
    anywhere = pl.BlockSpec(memory_space=pl.ANY)
    return pl.pallas_call(
        hand_over,
        name="hand_over",
        out_shape=tuple(jax.ShapeDtypeStruct((n, D), BF16) for n in (NODE, FINE, CE)),
        in_specs=[anywhere] * 3,
        out_specs=(hbm,) * 3,
        scratch_shapes=[pltpu.SemaphoreType.DMA((3,))],
        compiler_params=pltpu.CompilerParams(vmem_limit_bytes=1024 * 1024),
    )(*results)

def solution(mesh):
    rows = P(("group", "patch"), None)
    flat = P(("group", "patch"))
    in_specs = (rows, rows, rows, flat, flat, rows, flat, flat) + (P(),) * 8
    return jax.shard_map(
        functools.partial(call, True), mesh=mesh, in_specs=in_specs, out_specs=(rows, rows, rows), check_vma=False
    )
```

```python
import functools

import jax
import jax.numpy as jnp
from jax import lax
from jax.experimental import pallas as pl
from jax.experimental.pallas import tpu as pltpu
from jax.sharding import PartitionSpec as P

D = 512
NODE = 320
FINE = 2048
CE = 512
HALO = 64
COARSE = 16
LAYERS = 2
PAD = NODE + 2 * HALO
TABLE = PAD + NODE
GATHERED = 128 * COARSE
CHUNK = 2048
CHUNKS = FINE // CHUNK
COARSE_CHUNK = 512
EPSILON = 1e-05
F32 = jnp.float32
BF16 = jnp.bfloat16


def mm(a, b):
    return jnp.dot(a, b, preferred_element_type=F32)


def silu_half(pre):
    u = (pre * 0.5).astype(BF16)
    return u + u * jnp.tanh(u)


def centre(ref, l):
    weights = ref[l].astype(F32)
    ref[l] = (weights - jnp.mean(weights, axis=-1, keepdims=True)).astype(BF16)


def norm_rows(centred, gain_row):
    variance = jnp.mean(centred * centred, axis=-1, keepdims=True)
    return centred * lax.rsqrt(variance + EPSILON) * gain_row


def onehot(cond):
    return jnp.where(cond, 1.0, 0.0).astype(BF16)


def column(row):
    return jnp.transpose(jnp.broadcast_to(row, (128, 128)))


def kernel(
    h_hbm, fine_hbm, coarse_hbm, fs_hbm, fr_hbm, co_hbm, cr_hbm, cv_hbm,
    ef_hbm, eb_hbm, e2_hbm, eg_hbm, nf_hbm, nb_hbm, n2_hbm, ng_hbm,
    node_out, fine_out, coarse_out,
    L, ohT, CL, coh, crh, cohT, R, Wsr, W2, Nf, N2, H, halo, T, agg, pc, ps, pn,
    fs, fr, co, cr, cv, eb, eg, nb, ng,
    lsem, fsem, osem, ssem, rsem,
    *, comm,
):
    plan = [
        ("fs", fs_hbm, fs),
        ("fr", fr_hbm, fr),
        ("h", h_hbm, H.at[0]),
        ("wsr0", ef_hbm.at[0, pl.ds(D, 2 * D)], Wsr.at[0]),
        ("eb", eb_hbm, eb),
        ("r0", ef_hbm.at[0, pl.ds(0, D)], R.at[0, pl.ds(0, D)]),
        ("w2", e2_hbm, W2),
        ("eg", eg_hbm, eg),
        ("co", co_hbm, co),
        ("cr", cr_hbm, cr),
        ("cv", cv_hbm, cv),
        ("nf", nf_hbm, Nf),
        ("nb", nb_hbm, nb),
        ("coarse", coarse_hbm, CL),
        ("n2", n2_hbm, N2),
        ("ng", ng_hbm, ng),
        ("wsr1", ef_hbm.at[1, pl.ds(D, 2 * D)], Wsr.at[1]),
        ("r1", ef_hbm.at[1, pl.ds(0, D)], R.at[1, pl.ds(0, D)]),
    ]
    loads = {name: pltpu.make_async_copy(src, dst, lsem.at[k]) for k, (name, src, dst) in enumerate(plan)}

    def fine_load(i):
        rows = pl.ds(pl.multiple_of(i * CHUNK, CHUNK), CHUNK)
        return pltpu.make_async_copy(fine_hbm.at[rows], L.at[rows, pl.ds(0, D)], fsem.at[i])

    def start_loads():
        for name in ("fs", "fr", "h", "wsr0", "eb", "r0", "co", "cr", "cv", "coarse", "nf", "nb", "w2", "eg"):
            loads[name].start()
        for i in range(CHUNKS):
            fine_load(i).start()
        for name in ("n2", "ng", "wsr1", "r1"):
            loads[name].start()

    if comm:
        group = lax.axis_index("group")
        patch = lax.axis_index("patch")
        z, c = group // 2, group % 2
        x, y = patch // 4, patch % 4
        here = (x, y, z)

        def swap1(i):
            return i + 1 - 2 * (i % 2)

        def swap3(i):
            return 3 - i

        def cube(swap, order):
            targets = []
            for mask in order:
                tx, ty, tz = (swap(i) if mask >> k & 1 else i for k, i in enumerate(here))
                targets.append({"group": tz * 2 + c, "patch": tx * 4 + ty})
            return targets

        swaps = (swap1, swap3)
        stages = ((4,), (6, 2), (7, 5, 3, 1))
        first = [[cube(swaps[side], masks) for masks in stages] for side in range(2)]
        second = [cube(swaps[1 - side], (7, 6, 5, 3, 4, 2, 1)) for side in range(2)]
        partner = {"group": z * 2 + (1 - c), "patch": patch}
        following = {"group": group, "patch": (patch + 1) % 16}
        previous = {"group": group, "patch": (patch + 15) % 16}

        def bundle(side):
            pair = [(i + side) // 2 % 2 for i in here]
            return ((c * 2 + side) * 8 + pair[0] * 4 + pair[1] * 2 + pair[2]) * 64

        wx, wy, wz = (i % 2 for i in here)
        within = (wx * 4 + wy * 2 + wz) * 8
        pieces = (
            ((wx * 4 + wy * 2) * 8, 16),
            ((wx * 4 + (1 - wy) * 2) * 8, 16),
            ((1 - wx) * 32, 32),
        )

        def remote(l, k, src, dst, target):
            return pltpu.make_async_remote_copy(
                src_ref=src, dst_ref=dst, send_sem=ssem.at[l, (0, 1, 2, 2, 2, 2, 3)[k]], recv_sem=rsem.at[l, k],
                device_id=target, device_id_type=pl.DeviceIdType.MESH,
            )

        def same(l, k, start, count, target):
            ref = T.at[l, pl.ds(pl.multiple_of(start, 8), count)]
            return remote(l, k, ref, ref, target)

        def halos(l, source):
            return [
                remote(l, 0, source.at[pl.ds(NODE - HALO, HALO)], halo.at[l, pl.ds(0, HALO)], following),
                remote(l, 1, source.at[pl.ds(0, HALO)], halo.at[l, pl.ds(HALO, HALO)], previous),
            ]

        def own(l, side, source):
            dst = T.at[l, pl.ds(pl.multiple_of(bundle(side) + within, 8), 8)]
            return source.at[pl.ds(side * 8, 8)], dst

        def exchange(l):
            return same(l, 6, c * 1024, 1024, partner)

        barrier = pltpu.get_barrier_semaphore()
        peers = [*second[0], *second[1], partner, following, previous]
        for peer in peers:
            pl.semaphore_signal(barrier, inc=1, device_id=peer, device_id_type=pl.DeviceIdType.MESH)

        def begin(l, source):
            for k in range(3):
                for side in range(2):
                    for target in first[side][k]:
                        remote(l, 2 + k, *own(l, side, source), target).start()
            for side in range(2):
                pltpu.make_async_copy(*own(l, side, source), osem.at[l]).start()
            for copy in halos(l, source):
                copy.start()

        def step1(l, k):
            same(l, 2 + k, 0, 2 * len(stages[k]) * 8, partner).wait_recv()
            if k == 0:
                pltpu.make_async_copy(H.at[l, pl.ds(0, COARSE)], T.at[l, pl.ds(0, COARSE)], osem.at[l]).wait()
            start, count = pieces[k]
            for t in range(7):
                for side in range(2):
                    same(l, 5, bundle(side) + start, count, second[side][t]).start()

        def step2(l):
            same(l, 5, 0, 14 * 64, partner).wait_recv()
            exchange(l).start()

        def finish(l):
            exchange(l).wait_recv()

        def drain(l):
            same(l, 2, 0, 14 * 8 + 14 * 64, partner).wait_send()
            for copy in [*halos(l, H.at[l]), exchange(l)]:
                copy.wait_send()

        def wait_halos(l):
            for copy in halos(l, H.at[l]):
                copy.wait_recv()
    else:
        c = 0
        begin = step1 = step2 = finish = drain = wait_halos = lambda *a: None

    lane = lax.broadcasted_iota(jnp.int32, (128, 128), 1)
    row_node = lax.broadcasted_iota(jnp.int32, (NODE, 128), 0)

    def build_fine(k, carry):
        sender = column(fs[pl.ds(k, 1), :])
        receiver_row = fr[pl.ds(k, 1), :]
        receiver = column(receiver_row) + PAD
        rows = pl.ds(pl.multiple_of(k * 128, 128), 128)
        for b in range(TABLE // 128):
            at = lane + b * 128
            if b < 3:
                cond = sender == at
            elif b == 3:
                cond = (sender == at) | (receiver == at)
            else:
                cond = receiver == at
            L[rows, D + b * 128 : D + (b + 1) * 128] = onehot(cond)
        ohT[:, rows] = onehot(row_node == receiver_row)
        return carry

    def build_coarse(k, carry):
        owner = co[pl.ds(k, 1), :]
        row = cr[pl.ds(k, 1), :]
        oz, oc, ox, oy = owner >> 5, (owner >> 4) & 1, (owner >> 2) & 3, owner & 3
        side = row >> 3
        px, py, pz = (((i + side) >> 1) & 1 for i in (ox, oy, oz))
        place = ((px * 2 + py) * 2 + pz) * 8 + ((ox & 1) * 2 + (oy & 1)) * 2 + (oz & 1)
        sender = column(((oc * 2 + side) * 64 + place) * 8 + (row & 7))
        receiver_row = cv[pl.ds(k, 1), :]
        rows = pl.ds(pl.multiple_of(k * 128, 128), 128)
        for b in range(GATHERED // 128):
            coh[rows, b * 128 : (b + 1) * 128] = onehot(sender == lane + b * 128)
        crh[rows, :] = onehot(column(receiver_row) == lane)
        cohT[:, rows] = onehot(lax.broadcasted_iota(jnp.int32, (COARSE, 128), 0) == receiver_row)
        return carry

    if comm:
        pl.semaphore_wait(barrier, len(peers))
    begin(0, h_hbm)
    start_loads()
    for name in ("fs", "fr"):
        loads[name].wait()
    lax.fori_loop(0, FINE // 128, build_fine, 0)
    for name in ("h", "wsr0", "eb"):
        loads[name].wait()

    def fine_chunk(l, i):
        rows = pl.ds(pl.multiple_of(i * CHUNK, CHUNK), CHUNK)
        hidden = silu_half(mm(L[rows, :], R[l]))
        message = norm_rows(mm(hidden, W2[l]), eg[pl.ds(l, 1), :]).astype(BF16)
        L[rows, 0:D] += message
        agg[...] += mm(ohT[:, rows], message)

    def node_rows(l, start, count, received):
        rows = slice(start, start + count)
        hidden = silu_half(pn[rows] + mm(received.astype(BF16), Nf[l, D : 2 * D]))
        update = norm_rows(mm(hidden, N2[l]), ng[pl.ds(l, 1), :])
        H[l + 1, rows] = (H[l, rows].astype(F32) + update).astype(BF16)

    def layer(l, carry):
        latent = H[l]
        R[l, D + HALO : D + HALO + NODE] = mm(latent, Wsr[l, 0:D]).astype(BF16)
        R[l, D + PAD : D + TABLE] = (mm(latent, Wsr[l, D : 2 * D]) + eb[pl.ds(l, 1), :]).astype(BF16)
        agg[...] = jnp.zeros_like(agg)
        step1(l, 0)

        @pl.when(l == 0)
        def _():
            for name in ("r0", "co", "cr", "cv", "coarse", "nf", "nb"):
                loads[name].wait()
            lax.fori_loop(0, CE // 128, build_coarse, 0)

        pc[...] = mm(CL[...], R[l, 0:D]) + mm(crh[...], R[l, D + PAD : D + PAD + 128])
        pn[...] = mm(latent, Nf[l, 0:D]) + nb[pl.ds(l, 1), :]
        step1(l, 1)
        step1(l, 2)
        wait_halos(l)
        ends = mm(halo[l], Wsr[l, 0:D]).astype(BF16)
        R[l, D : D + HALO] = ends[0:HALO]
        R[l, D + HALO + NODE : D + PAD] = ends[HALO : 2 * HALO]

        @pl.when(l == 0)
        def _():
            for name in ("w2", "eg"):
                loads[name].wait()

        centre(W2, l)

        def chunk_step(i, inner):
            @pl.when(l == 0)
            def _():
                fine_load(i).wait()

            fine_chunk(l, i)

            @pl.when(l == LAYERS - 1)
            def _():
                rows = pl.ds(pl.multiple_of(i * CHUNK, CHUNK), CHUNK)
                fine_out[rows, :] = L[rows, 0:D]

            return inner

        lax.fori_loop(0, CHUNKS, chunk_step, 0)

        @pl.when(l == 0)
        def _():
            for name in ("n2", "ng", "wsr1", "r1"):
                loads[name].wait()

        centre(N2, l)
        node_rows(l, COARSE, NODE - COARSE, agg[COARSE:NODE])
        step2(l)
        mine = pl.ds(pl.multiple_of(c * 1024, 1024), 1024)
        other = pl.ds(pl.multiple_of((1 - c) * 1024, 1024), 1024)

        def first_half(k, inner):
            rows = pl.ds(pl.multiple_of(k * 256, 256), 256)
            ps[rows, :] = mm(coh[rows, mine], T[l, mine])
            return inner

        lax.fori_loop(0, CE // 256, first_half, 0)
        finish(l)
        received = agg[0:COARSE]
        messages = []
        for start in range(0, CE, COARSE_CHUNK):
            rows = slice(start, start + COARSE_CHUNK)
            sender = (ps[rows] + mm(coh[rows, other], T[l, other])).astype(BF16)
            hidden = silu_half(pc[rows] + mm(sender, Wsr[l, 0:D]))
            message = norm_rows(mm(hidden, W2[l]), eg[pl.ds(l, 1), :]).astype(BF16)
            received = received + mm(cohT[:, rows], message)
            messages.append(message)
        node_rows(l, 0, COARSE, received)

        @pl.when(l < LAYERS - 1)
        def _():
            begin(l + 1, H.at[l + 1])

        for k, message in enumerate(messages):
            CL[k * COARSE_CHUNK : (k + 1) * COARSE_CHUNK] += message
        drain(l)
        return carry

    lax.fori_loop(0, LAYERS, layer, 0)
    node_out[...] = H[LAYERS]
    coarse_out[...] = CL[...]


def hand_over(node, fine, coarse, node_out, fine_out, coarse_out, sem):
    copies = [
        pltpu.make_async_copy(src, dst, sem.at[k])
        for k, (src, dst) in enumerate(((fine, fine_out), (coarse, coarse_out), (node, node_out)))
    ]
    for copy in copies:
        copy.start()
    for copy in copies:
        copy.wait()


def call(comm, *args):
    (node, fine, coarse, fs, fr, co, cr, cv, ef, eb, e2, eg, nf, nb, n2, ng) = args
    hbm = pl.BlockSpec(memory_space=pltpu.HBM)
    vmem = pl.BlockSpec(memory_space=pltpu.VMEM)
    results = pl.pallas_call(
        functools.partial(kernel, comm=comm),
        name="processor",
        out_shape=tuple(pltpu.VMEM((n, D), BF16) for n in (NODE, FINE, CE)),
        in_specs=[hbm] * 16,
        out_specs=(vmem,) * 3,
        scratch_shapes=[
            pltpu.VMEM((FINE, D + TABLE), BF16),
            pltpu.VMEM((NODE, FINE), BF16),
            pltpu.VMEM((CE, D), BF16),
            pltpu.VMEM((CE, GATHERED), BF16),
            pltpu.VMEM((CE, 128), BF16),
            pltpu.VMEM((COARSE, CE), BF16),
            pltpu.VMEM((LAYERS, D + TABLE, D), BF16),
            pltpu.VMEM((LAYERS, 2 * D, D), BF16),
            pltpu.VMEM((LAYERS, D, D), BF16),
            pltpu.VMEM((LAYERS, 2 * D, D), BF16),
            pltpu.VMEM((LAYERS, D, D), BF16),
            pltpu.VMEM((LAYERS + 1, NODE, D), BF16),
            pltpu.VMEM((LAYERS, 2 * HALO, D), BF16),
            pltpu.VMEM((LAYERS, GATHERED, D), BF16),
            pltpu.VMEM((NODE, D), F32),
            pltpu.VMEM((CE, D), F32),
            pltpu.VMEM((CE, D), F32),
            pltpu.VMEM((NODE, D), F32),
            pltpu.VMEM((FINE // 128, 128), jnp.int32),
            pltpu.VMEM((FINE // 128, 128), jnp.int32),
            pltpu.VMEM((CE // 128, 128), jnp.int32),
            pltpu.VMEM((CE // 128, 128), jnp.int32),
            pltpu.VMEM((CE // 128, 128), jnp.int32),
            pltpu.VMEM((LAYERS, D), F32),
            pltpu.VMEM((LAYERS, D), F32),
            pltpu.VMEM((LAYERS, D), F32),
            pltpu.VMEM((LAYERS, D), F32),
            pltpu.SemaphoreType.DMA((18,)),
            pltpu.SemaphoreType.DMA((CHUNKS,)),
            pltpu.SemaphoreType.DMA((LAYERS,)),
            pltpu.SemaphoreType.DMA((LAYERS, 4)),
            pltpu.SemaphoreType.DMA((LAYERS, 7)),
        ],
        compiler_params=pltpu.CompilerParams(
            collective_id=0 if comm else None, has_side_effects=True, vmem_limit_bytes=56 * 1024 * 1024
        ),
    )(
        node, fine, coarse,
        fs.reshape(FINE // 128, 128), fr.reshape(FINE // 128, 128),
        co.reshape(CE // 128, 128), cr.reshape(CE // 128, 128), cv.reshape(CE // 128, 128),
        ef, eb, e2, eg, nf, nb, n2, ng,
    )
    anywhere = pl.BlockSpec(memory_space=pl.ANY)
    return pl.pallas_call(
        hand_over,
        name="hand_over",
        out_shape=tuple(jax.ShapeDtypeStruct((n, D), BF16) for n in (NODE, FINE, CE)),
        in_specs=[anywhere] * 3,
        out_specs=(hbm,) * 3,
        scratch_shapes=[pltpu.SemaphoreType.DMA((3,))],
        compiler_params=pltpu.CompilerParams(vmem_limit_bytes=1024 * 1024),
    )(*results)

def solution(mesh):
    rows = P(("group", "patch"), None)
    flat = P(("group", "patch"))
    in_specs = (rows, rows, rows, flat, flat, rows, flat, flat) + (P(),) * 8
    return jax.shard_map(
        functools.partial(call, True), mesh=mesh, in_specs=in_specs, out_specs=(rows, rows, rows), check_vma=False
    )
```
